128 devices in a mesh: damp: 4 (over z), front: 32 (over y, x, core).
Axes of the slice: x: 4, y: 4, z: 4, core: 2. Of those that a mesh axis runs over, the one named last changes fastest.
Arguments:
- base_front: float32 [4, 4096, 4096], P('damp', None, 'front'), as said below
- child_blocks: float32 [4, 2, 1024, 1024], P('damp', None, None, 'front'), as said below
- child_map: int32 [4, 2, 1024], P('damp'), may hold values from 0 to 4095, as said below
- src_index: int32 [2048], P('front'), may hold values from 0 to 4095
- src_amp: float32 [2048], P('front'), may hold values from -96 to 96
- rec_index: int32 [256], replicated, may hold values from 0 to 4095
- rec_resid: float32 [4, 256, 2048], P('damp', None, 'front'), may hold values from -96 to 96
- ancestor_field: float32 [4, 2, 3072, 2048], P('damp', None, None, 'front'), may hold values from -6 to 6
- damp_weight: float32 [4], P('damp'), may hold values from 0.05 to 0.5
Outputs:
- factored_front: float32 [4, 4096, 4096], P('damp', None, 'front')
- upward: float32 [4, 2, 3072, 2048], P('damp', None, None, 'front')
- pivot_field: float32 [4, 2, 1024, 2048], P('damp', None, None, 'front')
- gradient: float32 [1024], P('front')
The draws below stay inside these ranges and needn't reach their ends.
Inputs may be any that keep to these rules, and one draw needn't show every extreme that they name: `base_front`: symmetric in its last two dimensions, and the assembled front is positive definite. `child_blocks`: each child's block is symmetric. `child_map`: each child's 1024 indices are distinct and include 0 and 4095, in no particular order.
All inputs are finite; a program needn't handle non-finite values.
Results may differ from the reference program's by a relative error of at most 0.0003.
Values sent between devices are 32-bit elements; how exact they have to be, the bound alone decides.
No kernel may reach another device: no remote copies, remote signals or barrier semaphores. Data moves between devices by JAX's collectives and lax.ppermute only.
A program may use at most 192 MiB of HBM per device.

```python
import math
import jax
import jax.numpy as jnp
from jax import lax

ORDER = 4096
PIVOTS = 1024
CHILD = 1024
CHILDREN = 2
RECEIVERS = 256
SOURCES = 2048
N_DAMP = 4


def draw_base_front(key, part):
    noise = jax.random.uniform(jax.random.fold_in(key, 11), (N_DAMP, ORDER, ORDER), jnp.float32, -1.0, 1.0)
    symmetric = 0.5 * (noise + jnp.swapaxes(noise, 1, 2))
    edge = 2.0 * ((ORDER + CHILDREN * CHILD) / 6.0) ** 0.5
    diagonal = jax.random.uniform(jax.random.fold_in(key, 12), (N_DAMP, ORDER), jnp.float32, 1.3, 2.0) * edge
    identity = jnp.eye(ORDER, dtype=jnp.float32)
    result = symmetric * (1.0 - identity) + diagonal[:, :, None] * identity
    return result


def draw_child_blocks(key, part):
    noise = jax.random.uniform(jax.random.fold_in(key, 21), (N_DAMP, CHILDREN, CHILD, CHILD), jnp.float32, -1.0, 1.0)
    return 0.5 * (noise + jnp.swapaxes(noise, 2, 3))


def one_map(subkey):
    first_key, second_key = jax.random.split(subkey)
    chosen = jax.random.permutation(first_key, ORDER - 2)[:CHILD - 2] + 1
    ends = jnp.array([0, ORDER - 1], dtype=jnp.int32)
    joined = jnp.concatenate([ends, chosen.astype(jnp.int32)])
    return jax.random.permutation(second_key, joined)


def draw_child_map(key, part):
    subkeys = jax.random.split(jax.random.fold_in(key, 31), N_DAMP * CHILDREN)
    maps = jax.vmap(one_map)(subkeys)
    return maps.reshape(N_DAMP, CHILDREN, CHILD).astype(jnp.int32)


def set_ends(values, key, least, largest):
    index_at = [jax.random.randint(jax.random.fold_in(key, axis), (), 0, length) for axis, length in enumerate(values.shape)]
    longest = values.shape.index(max(values.shape))
    beside = index_at[:longest] + [(index_at[longest] + 1) % values.shape[longest]] + index_at[longest + 1:]
    return values.at[tuple(index_at)].set(least).at[tuple(beside)].set(largest)


def levels(stream_key, extent, shards, low, top_value):
    factor_of = 1.0
    for dim, parts in shards:
        heights = jax.random.uniform(jax.random.fold_in(jax.random.fold_in(stream_key, 6), dim), (parts,), jnp.float32, low / len(shards), top_value / len(shards))
        factor_of = factor_of * jnp.repeat(jnp.exp(heights), extent[dim] // parts).reshape((-1,) + (1,) * (len(extent) - 1 - dim))
    return factor_of


def gaussian(key, dims, width, limit, cuts=(), held_as=jnp.bfloat16):
    entries = width * jax.random.normal(key, dims, jnp.float32)
    if cuts:
        entries = entries * levels(key, dims, cuts, -0.22, 0.18)
    return jnp.clip(entries, -limit, limit).astype(held_as)


def setup_inputs(seed: int = 0) -> dict:
    arg_keys = jax.random.split(jax.random.key(seed), 10)
    return {
        "base_front": draw_base_front(jax.random.fold_in(arg_keys[9], 71), 0),
        "child_blocks": draw_child_blocks(jax.random.fold_in(arg_keys[9], 71), 0),
        "child_map": draw_child_map(jax.random.fold_in(arg_keys[9], 71), 0),
        "src_index": set_ends(jax.random.randint(arg_keys[3], (SOURCES,), 0, ORDER), jax.random.fold_in(arg_keys[3], 1), 0, ORDER - 1).astype(jnp.int32),
        "src_amp": gaussian(arg_keys[4], (SOURCES,), 16.0, 96.0, ((0, 32),), jnp.float32),
        "rec_index": set_ends(jax.random.randint(arg_keys[5], (RECEIVERS,), 0, ORDER), jax.random.fold_in(arg_keys[5], 1), 0, ORDER - 1).astype(jnp.int32),
        "rec_resid": gaussian(arg_keys[6], (N_DAMP, RECEIVERS, SOURCES), 16.0, 96.0, ((0, 4), (2, 32)), jnp.float32),
        "ancestor_field": gaussian(arg_keys[7], (N_DAMP, 2, ORDER - PIVOTS, SOURCES), 1.0, 6.0, ((0, 4), (3, 32)), jnp.float32),
        "damp_weight": jnp.clip(jnp.exp(math.log(0.5) - 2.3025851 * jax.random.uniform(arg_keys[8], (N_DAMP,), jnp.float32) ** levels(arg_keys[8], (N_DAMP,), ((0, 4),), -0.2, 0.2)), 0.05, 0.5),
    }


def reference(base_front, child_blocks, child_map, src_index, src_amp, rec_index, rec_resid, ancestor_field, damp_weight):
    highest = lax.Precision.HIGHEST
    factored_list = []
    upward_list = []
    pivot_list = []
    gradient = jnp.zeros((PIVOTS,), jnp.float32)
    columns = jnp.arange(SOURCES, dtype=jnp.int32)
    for group in range(N_DAMP):
        assembled = base_front[group]
        for child in range(CHILDREN):
            index_map = child_map[group, child]
            assembled = assembled.at[index_map[:, None], index_map[None, :]].add(child_blocks[group, child])
        lower_top = jnp.linalg.cholesky(assembled[:PIVOTS, :PIVOTS])
        lower_side = lax.linalg.triangular_solve(lower_top, assembled[PIVOTS:, :PIVOTS], left_side=False, lower=True, transpose_a=True)
        schur = assembled[PIVOTS:, PIVOTS:] - jnp.dot(lower_side, lower_side.T, precision=highest)
        left_part = jnp.concatenate([lower_top, lower_side], 0)
        right_part = jnp.concatenate([jnp.zeros((PIVOTS, ORDER - PIVOTS), jnp.float32), schur], 0)
        factored_list.append(jnp.concatenate([left_part, right_part], 1))
        forward = jnp.zeros((ORDER, SOURCES), jnp.float32).at[src_index, columns].set(src_amp)
        adjoint = jnp.zeros((ORDER, SOURCES), jnp.float32).at[rec_index].add(rec_resid[group])
        rhs = jnp.concatenate([forward, adjoint], 1)
        solved_top = lax.linalg.triangular_solve(lower_top, rhs[:PIVOTS], left_side=True, lower=True)
        passed = rhs[PIVOTS:] - jnp.dot(lower_side, solved_top, precision=highest)
        above = jnp.concatenate([ancestor_field[group, 0], ancestor_field[group, 1]], 1)
        inner = solved_top - jnp.dot(lower_side.T, above, precision=highest)
        pivot_all = lax.linalg.triangular_solve(lower_top, inner, left_side=True, lower=True, transpose_a=True)
        upward_list.append(jnp.stack([passed[:, :SOURCES], passed[:, SOURCES:]]))
        pivot_list.append(jnp.stack([pivot_all[:, :SOURCES], pivot_all[:, SOURCES:]]))
        gradient = gradient + damp_weight[group] * jnp.sum(pivot_all[:, :SOURCES] * pivot_all[:, SOURCES:], axis=1)
    return (jnp.stack(factored_list), jnp.stack(upward_list), jnp.stack(pivot_list), gradient)
```

```python
import functools

import jax
import jax.numpy as jnp
from jax import lax
from jax.experimental import pallas as pl
from jax.experimental.pallas import tpu as pltpu
from jax.sharding import PartitionSpec as P

ORDER = 4096
PIVOTS = 1024
REST = ORDER - PIVOTS
BLOCK = 128
SIDE = 4


def split(a):
    hi = a.astype(jnp.bfloat16)
    lo = (a - hi.astype(jnp.float32)).astype(jnp.bfloat16)
    return hi, lo


def dg(a, b, ca, cb):
    return lax.dot_general(a, b, (((ca,), (cb,)), ((), ())), preferred_element_type=jnp.float32)


def mm(a, b, ca=1, cb=0):
    return dg(a[0], b[0], ca, cb) + (dg(a[0], b[1], ca, cb) + dg(a[1], b[0], ca, cb))


def front_perm(shift, along_x_core):
    pairs = []
    for y in range(SIDE):
        for x in range(SIDE):
            for c in range(2):
                dy, dx = (0, shift) if c == along_x_core else (shift, 0)
                to = ((y + dy) % SIDE) * 8 + ((x + dx) % SIDE) * 2 + c
                pairs.append((y * 8 + x * 2 + c, to))
    return pairs


PARTNER = [(i, i ^ 1) for i in range(32)]


def send(v, pairs):
    return lax.ppermute(v, "front", pairs)


def ring(v, along_x_core):
    back, two, on = (send(v, front_perm(s, along_x_core)) for s in (-1, 2, 1))
    return [v, back, two, on]


def spread(v):
    bundle = jnp.stack(ring(v, 0))
    own = ring(bundle, 1)
    return own + [send(b, PARTNER) for b in own]


def place(pos, which, e, d):
    core, x, y = pos % 2, (pos // 2) % SIDE, pos // 8
    if which:
        core = 1 - core
    first = core == 0
    yy = (y + jnp.where(first, e, d)) % SIDE
    xx = (x + jnp.where(first, d, e)) % SIDE
    return yy * 8 + xx * 2 + core


def fetch(pos, bundles, target, sems):
    copies = []
    for which in range(2):
        for e in range(SIDE):
            for d in range(SIDE):
                n = which * 16 + e * 4 + d
                f = place(pos, which, e, d)
                copy = pltpu.make_async_copy(bundles[which * 4 + e].at[d], target(f), sems.at[n])
                copy.start()
                copies.append(copy)
    for copy in copies:
        copy.wait()


ANY = pl.BlockSpec(memory_space=pl.ANY)
VMEM = pl.BlockSpec(memory_space=pltpu.VMEM)
SMEM = pl.BlockSpec(memory_space=pltpu.SMEM)


def f32(*shape):
    return jax.ShapeDtypeStruct(shape, jnp.float32)


def picked(map_row, first, count, block):
    rows = lax.broadcasted_iota(jnp.int32, (count, 1024), 0) + first
    take = (map_row == rows).astype(jnp.bfloat16)
    hi = jnp.zeros((count, 1024), jnp.float32)
    lo = jnp.zeros((count, 1024), jnp.float32)
    for k in range(0, 1024, 256):
        bh, bl = split(block[k : k + 256, :])
        hi = hi + dg(take[:, k : k + 256], bh, 1, 0)
        lo = lo + dg(take[:, k : k + 256], bl, 1, 0)
    return hi.astype(jnp.bfloat16), lo.astype(jnp.bfloat16)


def pivot_rows_kernel(pos_ref, map_ref, base_ref, *refs):
    bundles, (out_ref, blocks, sems) = refs[:8], refs[8:]
    pos = pos_ref[0]
    fetch(pos, bundles, lambda f: blocks.at[:, pl.ds(pl.multiple_of(f * 32, 32), 32), :], sems)
    total = base_ref[...]
    for child in range(2):
        map_row = map_ref[child : child + 1, :]
        hi, lo = picked(map_row, pos * 32, 32, blocks.at[child])
        where = (map_row == lax.broadcasted_iota(jnp.int32, (PIVOTS, 1024), 0)).astype(jnp.bfloat16)
        total = total + (dg(hi, where, 1, 1) + dg(lo, where, 1, 1))
    out_ref[...] = total


def pivot_rows(pos, maps, base_rows, bundles):
    return pl.pallas_call(
        pivot_rows_kernel,
        out_shape=f32(32, PIVOTS),
        in_specs=[SMEM, VMEM, VMEM] + [ANY] * 8,
        out_specs=VMEM,
        scratch_shapes=[pltpu.VMEM((2, 1024, 1024), jnp.float32), pltpu.SemaphoreType.DMA((32,))],
        compiler_params=pltpu.CompilerParams(vmem_limit_bytes=40 << 20),
        cost_estimate=pl.CostEstimate(flops=2 * 10**9, bytes_accessed=9 << 20, transcendentals=0),
        name="pivot_rows",
    )(pos, maps, base_rows, *bundles)


def columns_kernel(pos_ref, map_ref, base_ref, *refs):
    bundles, (out_ref, blocks, sems) = refs[:8], refs[8:]
    pos = pos_ref[0]
    fetch(pos, bundles, lambda f: blocks.at[:, pl.ds(pl.multiple_of(f * 32, 32), 32), :], sems)
    parts = []
    for child in range(2):
        hi, lo = picked(map_ref[child : child + 1, :], pos * BLOCK, BLOCK, blocks.at[child])
        parts.append(jnp.concatenate([hi, lo], 0))
    tall = 512

    def chunk(i, _):
        row = pl.multiple_of(i * tall, tall)
        rows = lax.broadcasted_iota(jnp.int32, (tall, 1024), 0) + row
        total = None
        for child in range(2):
            where = (map_ref[child : child + 1, :] == rows).astype(jnp.bfloat16)
            term = dg(where, parts[child], 1, 1)
            total = term if total is None else total + term
        out_ref[pl.ds(row, tall), :] = base_ref[pl.ds(row, tall), :] + (total[:, :BLOCK] + total[:, BLOCK:])
        return 0

    lax.fori_loop(0, ORDER // tall, chunk, 0)


def columns(pos, maps, base_cols, bundles):
    return pl.pallas_call(
        columns_kernel,
        out_shape=f32(ORDER, BLOCK),
        in_specs=[SMEM, VMEM, VMEM] + [ANY] * 8,
        out_specs=VMEM,
        scratch_shapes=[pltpu.VMEM((2, 1024, 1024), jnp.float32), pltpu.SemaphoreType.DMA((32,))],
        compiler_params=pltpu.CompilerParams(vmem_limit_bytes=48 << 20),
        cost_estimate=pl.CostEstimate(flops=6 * 10**9, bytes_accessed=12 << 20, transcendentals=0),
        name="columns",
    )(pos, maps, base_cols, *bundles)


def factor_block(block):
    tiles = BLOCK // 8
    left = [block[8 * r : 8 * r + 8, :] for r in range(tiles)]
    lane = lax.broadcasted_iota(jnp.int32, (8, BLOCK), 1)
    sub = lax.broadcasted_iota(jnp.int32, (8, BLOCK), 0)
    right = [(lane == sub + 8 * r).astype(jnp.float32) for r in range(tiles)]

    def wide(x):
        return jnp.broadcast_to(x, (8, BLOCK))

    for top in range(tiles):
        first = 8 * top
        cols = [[wide(left[r][:, first + q : first + q + 1]) for r in range(top, tiles)] for q in range(8)]
        rows = [wide(left[top][q : q + 1, :]) for q in range(8)]
        inv = [wide(right[top][q : q + 1, :]) for q in range(8)]
        low = {(i, q): wide(cols[q][0][i : i + 1, :]) for i in range(8) for q in range(i + 1)}
        scale = []
        for q in range(8):
            scale.append(lax.rsqrt(low[q, q]))
            for i in range(q + 1, 8):
                low[i, q] = low[i, q] * scale[q]
            for i in range(q + 1, 8):
                for n in range(q + 1, i + 1):
                    low[i, n] = low[i, n] - low[i, q] * low[n, q]
        for q in range(8):
            for n in range(q):
                rows[q] = rows[q] - low[q, n] * rows[n]
                inv[q] = inv[q] - low[q, n] * inv[n]
            rows[q] = rows[q] * scale[q]
            inv[q] = inv[q] * scale[q]
        for r in range(top + 1, tiles):
            factors = []
            for q in range(8):
                t = cols[q][r - top]
                for n in range(q):
                    t = t - factors[n] * low[q, n]
                factors.append(t * scale[q])
            for q in range(8):
                left[r] = left[r] - factors[q] * rows[q]
                right[r] = right[r] - factors[q] * inv[q]
        for q in range(8):
            left[top] = jnp.where(sub == q, rows[q], left[top])
            right[top] = jnp.where(sub == q, inv[q], right[top])
    return jnp.concatenate(left, 0), jnp.concatenate(right, 0)


def cholesky(m, l_ref, w_ref, lh, ll, vh, vl):
    w_ref[...] = jnp.zeros_like(w_ref)
    l_ref[...] = jnp.zeros_like(l_ref)
    row = lax.broadcasted_iota(jnp.int32, (BLOCK, BLOCK), 0)
    col = lax.broadcasted_iota(jnp.int32, (BLOCK, BLOCK), 1)
    panels = PIVOTS // BLOCK

    def step(k, _):
        at = pl.ds(pl.multiple_of(k * BLOCK, BLOCK), BLOCK)
        upper, inv = factor_block(m[at, at])
        inv = jnp.where(row >= col, inv, 0.0)
        l_ref[at, at] = jnp.where(row >= col, upper.T, 0.0)
        w_ref[at, at] = inv
        vh[...], vl[...] = split(inv)
        for kk in range(panels - 1):

            @pl.when(k == kk)
            def _():
                a, b = kk * BLOCK, (kk + 1) * BLOCK
                below = mm(split(m[b:, a:b]), (vh[...], vl[...]), 1, 1)
                l_ref[b:, a:b] = below
                lh[b:, a:b], ll[b:, a:b] = split(below)
                ahead = slice(b, b + BLOCK)
                m[b:, ahead] = m[b:, ahead] - mm((lh[b:, :b], ll[b:, :b]), (lh[ahead, :b], ll[ahead, :b]), 1, 1)

        return 0

    lax.fori_loop(0, panels, step, 0)
    for s in (128, 256, 512):
        for a in range(0, PIVOTS, 2 * s):
            up, dn = slice(a, a + s), slice(a + s, a + 2 * s)
            inner = mm((lh[dn, up], ll[dn, up]), split(w_ref[up, up]))
            w_ref[dn, up] = -mm(split(w_ref[dn, dn]), split(inner))


def factor_kernel(pos_ref, cols_ref, rhs_ref, *refs):
    bundles, (w_ref, top_ref, y1_ref, zx_ref, m, l_ref, lh, ll, vh, vl, sems) = refs[:8], refs[8:]
    pos = pos_ref[0]
    fetch(pos, bundles, lambda f: m.at[pl.ds(pl.multiple_of(f * 32, 32), 32), :], sems)
    cholesky(m, l_ref, w_ref, lh, ll, vh, vl)
    lh[...], ll[...] = split(w_ref[...])
    inv = (lh[...], ll[...])
    both = jnp.concatenate([rhs_ref[...], cols_ref[...].T], 0)
    solved = mm(split(both), inv, 1, 1)
    y1_ref[...] = solved[:BLOCK]
    zx_ref[...] = mm(split(solved), inv)
    own = pos < PIVOTS // BLOCK

    @pl.when(own)
    def _():
        at = pl.ds(pl.multiple_of(pos * BLOCK, BLOCK), BLOCK)
        zx_ref[BLOCK:, :] = -w_ref[at, :]
        top_ref[...] = l_ref[:, at]

    @pl.when(jnp.logical_not(own))
    def _():
        top_ref[...] = jnp.zeros_like(top_ref)


def factor(pos, cols_top, rhs_top, bundles):
    return pl.pallas_call(
        factor_kernel,
        out_shape=(f32(PIVOTS, PIVOTS), f32(PIVOTS, BLOCK), f32(BLOCK, PIVOTS), f32(2 * BLOCK, PIVOTS)),
        in_specs=[SMEM, VMEM, VMEM] + [ANY] * 8,
        out_specs=(VMEM,) * 4,
        scratch_shapes=[pltpu.VMEM((PIVOTS, PIVOTS), jnp.float32)] * 2
        + [pltpu.VMEM((PIVOTS, PIVOTS), jnp.bfloat16)] * 2
        + [pltpu.VMEM((BLOCK, BLOCK), jnp.bfloat16)] * 2
        + [pltpu.SemaphoreType.DMA((32,))],
        compiler_params=pltpu.CompilerParams(vmem_limit_bytes=48 << 20),
        cost_estimate=pl.CostEstimate(flops=40 * 10**9, bytes_accessed=16 << 20, transcendentals=0),
        name="factor",
    )(pos, cols_top, rhs_top, *bundles)


def load_rest(tops_ref, rest, sems):
    copies = []
    for n in range(REST // BLOCK):
        copy = pltpu.make_async_copy(
            tops_ref.at[PIVOTS // BLOCK + n], rest.at[:, n * BLOCK : (n + 1) * BLOCK], sems.at[n]
        )
        copy.start()
        copies.append(copy)
    return copies


WIDE = 512


def pivot_kernel(weight_ref, above_ref, y1_ref, w_ref, tops_ref, field_ref, terms_ref, rest, sems):
    copies = load_rest(tops_ref, rest, sems)
    total = jnp.zeros((BLOCK, PIVOTS), jnp.float32)
    per = WIDE // BLOCK
    for n in range(REST // WIDE):
        for copy in copies[n * per : (n + 1) * per]:
            copy.wait()
        at = slice(n * WIDE, (n + 1) * WIDE)
        total = total + mm(split(above_ref[:, at]), split(rest[:, at]), 1, 1)
    inv = split(w_ref[...])
    inner = y1_ref[...] - mm(split(total), inv, 1, 1)
    field = mm(split(inner), inv)
    field_ref[...] = field
    half = BLOCK // 2
    terms_ref[...] = weight_ref[0] * jnp.sum(field[:half] * field[half:], axis=0, keepdims=True)


def pivot(weight, above, y1, w, tops):
    return pl.pallas_call(
        pivot_kernel,
        out_shape=(f32(BLOCK, PIVOTS), f32(1, PIVOTS)),
        in_specs=[SMEM, VMEM, VMEM, VMEM, ANY],
        out_specs=(VMEM, VMEM),
        scratch_shapes=[pltpu.VMEM((PIVOTS, REST), jnp.float32), pltpu.SemaphoreType.DMA((REST // BLOCK,))],
        compiler_params=pltpu.CompilerParams(vmem_limit_bytes=52 << 20),
        cost_estimate=pl.CostEstimate(flops=6 * 10**9, bytes_accessed=20 << 20, transcendentals=0),
        name="pivot",
    )(weight, above, y1, w, tops)


def rest_kernel(pos_ref, cols_ref, top_ref, rhs_ref, zx_ref, tops_ref, front_ref, up_ref, rest, sems):
    copies = load_rest(tops_ref, rest, sems)
    front_ref[:PIVOTS, :] = top_ref[...]
    own = pos_ref[0] < PIVOTS // BLOCK
    zx = split(zx_ref[...])
    per = WIDE // BLOCK
    for n in range(REST // WIDE):
        for copy in copies[n * per : (n + 1) * per]:
            copy.wait()
        at = slice(n * WIDE, (n + 1) * WIDE)
        down = slice(PIVOTS + n * WIDE, PIVOTS + (n + 1) * WIDE)
        out = mm(zx, split(rest[:, at]))
        up_ref[:, at] = rhs_ref[:, down] - out[:BLOCK]
        front_ref[down, :] = jnp.where(own, 0.0, cols_ref[down, :]) - out[BLOCK:].T


def finish(pos, cols, top, rhs, zx, tops):
    return pl.pallas_call(
        rest_kernel,
        out_shape=(f32(ORDER, BLOCK), f32(BLOCK, REST)),
        in_specs=[SMEM, VMEM, VMEM, VMEM, VMEM, ANY],
        out_specs=(VMEM, VMEM),
        scratch_shapes=[pltpu.VMEM((PIVOTS, REST), jnp.float32), pltpu.SemaphoreType.DMA((REST // BLOCK,))],
        compiler_params=pltpu.CompilerParams(vmem_limit_bytes=52 << 20),
        cost_estimate=pl.CostEstimate(flops=6 * 10**9, bytes_accessed=20 << 20, transcendentals=0),
        name="finish",
    )(pos, cols, top, rhs, zx, tops)


def axis_perm(shift, dy, dx):
    pairs = []
    for y in range(SIDE):
        for x in range(SIDE):
            for c in range(2):
                to = ((y + dy * shift) % SIDE) * 8 + ((x + dx * shift) % SIDE) * 2 + c
                pairs.append((y * 8 + x * 2 + c, to))
    return pairs


def sum_all(v):
    v = v + send(v, PARTNER)
    for dy, dx in ((0, 1), (1, 0)):
        one, two, three = (send(v, axis_perm(s, dy, dx)) for s in (1, 2, 3))
        v = (v + two) + (one + three)
    one, two, three = (lax.ppermute(v, "damp", [(i, (i + s) % 4) for i in range(4)]) for s in (1, 2, 3))
    return (v + two) + (one + three)


def per_device(
    base_front,
    child_blocks,
    child_map,
    src_index,
    src_amp,
    rec_index,
    rec_resid,
    ancestor_field,
    damp_weight,
):
    position = lax.axis_index("front")
    pos = position.reshape(1).astype(jnp.int32)
    base = base_front[0]
    maps = child_map[0]
    bundles = spread(jnp.swapaxes(child_blocks[0], 1, 2))
    base_t = base[:PIVOTS].T
    base_rows = 0.0
    for r in range(4):
        base_rows = base_rows + send(base_t[32 * r : 32 * r + 32], [(j, 4 * j + r) for j in range(8)])
    rows = pivot_rows(pos, maps, base_rows, bundles)
    cols = columns(pos, maps, base, bundles)
    tops = lax.all_gather(cols[:PIVOTS], "front", axis=0)
    ids = jnp.arange(ORDER, dtype=jnp.int32)
    forward = jnp.where(src_index[:, None] == ids[None, :], src_amp[:, None], 0.0)
    table = (rec_index[:, None] == ids[None, :]).astype(jnp.float32)
    adjoint = lax.dot_general(
        rec_resid[0], table, (((0,), (0,)), ((), ())), precision=lax.Precision.HIGHEST
    )
    rhs = jnp.concatenate([forward, adjoint], 0)
    above = jnp.swapaxes(ancestor_field[0], 1, 2).reshape(BLOCK, REST)
    w, top, y1, zx = factor(pos, cols[:PIVOTS], rhs[:, :PIVOTS], spread(rows))
    field, terms = pivot(damp_weight, above, y1, w, tops)
    summed = sum_all(terms.reshape(8, BLOCK))
    factored, up = finish(pos, cols, top, rhs, zx, tops)
    gradient = lax.dynamic_slice_in_dim(summed.reshape(PIVOTS), position * 32, 32, 0)
    upward = jnp.swapaxes(up.reshape(2, BLOCK // 2, REST), 1, 2)
    pivot_field = jnp.swapaxes(field.reshape(2, BLOCK // 2, PIVOTS), 1, 2)
    return (factored[None], upward[None], pivot_field[None], gradient)


def solution(mesh):
    return jax.shard_map(
        per_device,
        mesh=mesh,
        in_specs=(
            P("damp", None, "front"),
            P("damp", None, None, "front"),
            P("damp", None, None),
            P("front"),
            P("front"),
            P(),
            P("damp", None, "front"),
            P("damp", None, None, "front"),
            P("damp"),
        ),
        out_specs=(
            P("damp", None, "front"),
            P("damp", None, None, "front"),
            P("damp", None, None, "front"),
            P("front"),
        ),
        check_vma=False,
    )
```

```python
import functools

import jax
import jax.numpy as jnp
from jax import lax
from jax.experimental import pallas as pl
from jax.experimental.pallas import tpu as pltpu
from jax.sharding import PartitionSpec as P

ORDER = 4096
PIVOTS = 1024
REST = ORDER - PIVOTS
BLOCK = 128
SIDE = 4


def split(a):
    hi = a.astype(jnp.bfloat16)
    lo = (a - hi.astype(jnp.float32)).astype(jnp.bfloat16)
    return hi, lo


def dg(a, b, ca, cb):
    return lax.dot_general(a, b, (((ca,), (cb,)), ((), ())), preferred_element_type=jnp.float32)


def mm(a, b, ca=1, cb=0):
    return dg(a[0], b[0], ca, cb) + (dg(a[0], b[1], ca, cb) + dg(a[1], b[0], ca, cb))


def front_perm(shift, along_x_core):
    pairs = []
    for y in range(SIDE):
        for x in range(SIDE):
            for c in range(2):
                dy, dx = (0, shift) if c == along_x_core else (shift, 0)
                to = ((y + dy) % SIDE) * 8 + ((x + dx) % SIDE) * 2 + c
                pairs.append((y * 8 + x * 2 + c, to))
    return pairs


PARTNER = [(i, i ^ 1) for i in range(32)]


def send(v, pairs):
    return lax.ppermute(v, "front", pairs)


def ring(v, along_x_core):
    back, two, on = (send(v, front_perm(s, along_x_core)) for s in (-1, 2, 1))
    return [v, back, two, on]


def spread(v):
    bundle = jnp.stack(ring(v, 0))
    own = ring(bundle, 1)
    return own + [send(b, PARTNER) for b in own]


def place(pos, which, e, d):
    core, x, y = pos % 2, (pos // 2) % SIDE, pos // 8
    if which:
        core = 1 - core
    first = core == 0
    yy = (y + jnp.where(first, e, d)) % SIDE
    xx = (x + jnp.where(first, d, e)) % SIDE
    return yy * 8 + xx * 2 + core


def fetch(pos, bundles, target, sems):
    copies = []
    for which in range(2):
        for e in range(SIDE):
            for d in range(SIDE):
                n = which * 16 + e * 4 + d
                f = place(pos, which, e, d)
                copy = pltpu.make_async_copy(bundles[which * 4 + e].at[d], target(f), sems.at[n])
                copy.start()
                copies.append(copy)
    for copy in copies:
        copy.wait()


ANY = pl.BlockSpec(memory_space=pl.ANY)
VMEM = pl.BlockSpec(memory_space=pltpu.VMEM)
SMEM = pl.BlockSpec(memory_space=pltpu.SMEM)


def f32(*shape):
    return jax.ShapeDtypeStruct(shape, jnp.float32)


PACKED = 5 * BLOCK


def pack(block):
    start = lax.axis_index("front") // 4 * BLOCK
    twice = jnp.concatenate([block, block[:, :, : PACKED - BLOCK]], 2)
    return lax.dynamic_slice_in_dim(twice, start, PACKED, 2)


def picked(map_row, first, count, block):
    rows = lax.broadcasted_iota(jnp.int32, (count, 1024), 0) + first
    take = (map_row == rows).astype(jnp.bfloat16)
    panels = [take[:, BLOCK * i : BLOCK * (i + 1)] for i in range(8)]
    sums = [[None] * 8, [None] * 8]

    def put(part, j, term):
        old = sums[part][j]
        sums[part][j] = term if old is None else old + term

    for i in range(8):
        ahead = jnp.concatenate([panels[(i + t) % 8] for t in (1, 2, 3)], 1)
        for part, held in enumerate(split(block[BLOCK * i : BLOCK * (i + 1), :])):
            straight = dg(panels[i], held, 1, 0)
            for t in range(5):
                put(part, (i + t) % 8, straight[:, BLOCK * t : BLOCK * (t + 1)])
            put(part, i, dg(ahead, held[:, BLOCK : 4 * BLOCK], 1, 1))
    return tuple(jnp.concatenate(p, 1).astype(jnp.bfloat16) for p in sums)


def fetch_children(pos, bundles, blocks, sems):
    fetch(pos, bundles, lambda f: blocks.at[:, pl.ds(pl.multiple_of(f * 32, 32), 32), :], sems)


def pivot_rows_kernel(pos_ref, map_ref, base_ref, *refs):
    bundles, (out_ref, blocks, sems) = refs[:8], refs[8:]
    pos = pos_ref[0]
    fetch_children(pos, bundles, blocks, sems)
    total = base_ref[...]
    for child in range(2):
        map_row = map_ref[child : child + 1, :]
        hi, lo = picked(map_row, pos * 32, 32, blocks.at[child])
        where = (map_row == lax.broadcasted_iota(jnp.int32, (PIVOTS, 1024), 0)).astype(jnp.bfloat16)
        total = total + (dg(hi, where, 1, 1) + dg(lo, where, 1, 1))
    out_ref[...] = total


CHILD_SCRATCH = [pltpu.VMEM((2, 1024, PACKED), jnp.float32), pltpu.SemaphoreType.DMA((32,))]


def pivot_rows(pos, maps, base_rows, bundles):
    return pl.pallas_call(
        pivot_rows_kernel,
        out_shape=f32(32, PIVOTS),
        in_specs=[SMEM, VMEM, VMEM] + [ANY] * 8,
        out_specs=VMEM,
        scratch_shapes=CHILD_SCRATCH,
        compiler_params=pltpu.CompilerParams(vmem_limit_bytes=32 << 20),
        cost_estimate=pl.CostEstimate(flops=2 * 10**9, bytes_accessed=6 << 20, transcendentals=0),
        name="pivot_rows",
    )(pos, maps, base_rows, *bundles)


def columns_kernel(pos_ref, map_ref, base_ref, *refs):
    bundles, (top_ref, rest_ref, blocks, sems) = refs[:8], refs[8:]
    pos = pos_ref[0]
    fetch_children(pos, bundles, blocks, sems)
    parts = []
    for child in range(2):
        hi, lo = picked(map_ref[child : child + 1, :], pos * BLOCK, BLOCK, blocks.at[child])
        parts.append(jnp.concatenate([hi, lo], 0))
    tall = 512

    def chunk(out_ref, skip, i):
        at = pl.multiple_of(i * tall, tall)
        rows = lax.broadcasted_iota(jnp.int32, (tall, 1024), 0) + (at + skip)
        total = None
        for child in range(2):
            where = (map_ref[child : child + 1, :] == rows).astype(jnp.bfloat16)
            term = dg(where, parts[child], 1, 1)
            total = term if total is None else total + term
        out_ref[pl.ds(at, tall), :] = base_ref[pl.ds(at + skip, tall), :] + (total[:, :BLOCK] + total[:, BLOCK:])
        return 0

    lax.fori_loop(0, PIVOTS // tall, lambda i, _: chunk(top_ref, 0, i), 0)
    lax.fori_loop(0, REST // tall, lambda i, _: chunk(rest_ref, PIVOTS, i), 0)


def columns(pos, maps, base_cols, bundles):
    return pl.pallas_call(
        columns_kernel,
        out_shape=(f32(PIVOTS, BLOCK), f32(REST, BLOCK)),
        in_specs=[SMEM, VMEM, VMEM] + [ANY] * 8,
        out_specs=(VMEM, VMEM),
        scratch_shapes=CHILD_SCRATCH,
        compiler_params=pltpu.CompilerParams(vmem_limit_bytes=40 << 20),
        cost_estimate=pl.CostEstimate(flops=6 * 10**9, bytes_accessed=10 << 20, transcendentals=0),
        name="columns",
    )(pos, maps, base_cols, *bundles)


def factor_block(block):
    tiles = BLOCK // 8
    left = [block[8 * r : 8 * r + 8, :] for r in range(tiles)]
    lane = lax.broadcasted_iota(jnp.int32, (8, BLOCK), 1)
    sub = lax.broadcasted_iota(jnp.int32, (8, BLOCK), 0)
    right = [(lane == sub + 8 * r).astype(jnp.float32) for r in range(tiles)]

    def wide(x):
        return jnp.broadcast_to(x, (8, BLOCK))

    for top in range(tiles):
        first = 8 * top
        cols = [[wide(left[r][:, first + q : first + q + 1]) for r in range(top, tiles)] for q in range(8)]
        rows = [wide(left[top][q : q + 1, :]) for q in range(8)]
        inv = [wide(right[top][q : q + 1, :]) for q in range(8)]
        low = {(i, q): wide(cols[q][0][i : i + 1, :]) for i in range(8) for q in range(i + 1)}
        scale = []
        for q in range(8):
            scale.append(lax.rsqrt(low[q, q]))
            for i in range(q + 1, 8):
                low[i, q] = low[i, q] * scale[q]
            for i in range(q + 1, 8):
                for n in range(q + 1, i + 1):
                    low[i, n] = low[i, n] - low[i, q] * low[n, q]
        for q in range(8):
            for n in range(q):
                rows[q] = rows[q] - low[q, n] * rows[n]
                inv[q] = inv[q] - low[q, n] * inv[n]
            rows[q] = rows[q] * scale[q]
            inv[q] = inv[q] * scale[q]
        for r in range(top + 1, tiles):
            factors = []
            for q in range(8):
                t = cols[q][r - top]
                for n in range(q):
                    t = t - factors[n] * low[q, n]
                factors.append(t * scale[q])
            for q in range(8):
                left[r] = left[r] - factors[q] * rows[q]
                right[r] = right[r] - factors[q] * inv[q]
        for q in range(8):
            left[top] = jnp.where(sub == q, rows[q], left[top])
            right[top] = jnp.where(sub == q, inv[q], right[top])
    return jnp.concatenate(left, 0), jnp.concatenate(right, 0)


def cholesky(m, l_ref, w_ref, lh, ll, vh, vl):
    w_ref[...] = jnp.zeros_like(w_ref)
    l_ref[...] = jnp.zeros_like(l_ref)
    row = lax.broadcasted_iota(jnp.int32, (BLOCK, BLOCK), 0)
    col = lax.broadcasted_iota(jnp.int32, (BLOCK, BLOCK), 1)
    panels = PIVOTS // BLOCK

    def step(k, _):
        at = pl.ds(pl.multiple_of(k * BLOCK, BLOCK), BLOCK)
        upper, inv = factor_block(m[at, at])
        inv = jnp.where(row >= col, inv, 0.0)
        l_ref[at, at] = jnp.where(row >= col, upper.T, 0.0)
        w_ref[at, at] = inv
        vh[...], vl[...] = split(inv)
        for kk in range(panels - 1):

            @pl.when(k == kk)
            def _():
                a, b = kk * BLOCK, (kk + 1) * BLOCK
                below = mm(split(m[b:, a:b]), (vh[...], vl[...]), 1, 1)
                l_ref[b:, a:b] = below
                lh[b:, a:b], ll[b:, a:b] = split(below)
                ahead = slice(b, b + BLOCK)
                m[b:, ahead] = m[b:, ahead] - mm((lh[b:, :b], ll[b:, :b]), (lh[ahead, :b], ll[ahead, :b]), 1, 1)

        return 0

    lax.fori_loop(0, panels, step, 0)
    for s in (128, 256, 512):
        for a in range(0, PIVOTS, 2 * s):
            up, dn = slice(a, a + s), slice(a + s, a + 2 * s)
            inner = mm((lh[dn, up], ll[dn, up]), split(w_ref[up, up]))
            w_ref[dn, up] = -mm(split(w_ref[dn, dn]), split(inner))


def factor_kernel(pos_ref, cols_ref, rhs_ref, *refs):
    bundles, (w_ref, top_ref, y1_ref, zx_ref, m, l_ref, lh, ll, vh, vl, sems) = refs[:8], refs[8:]
    pos = pos_ref[0]
    fetch(pos, bundles, lambda f: m.at[pl.ds(pl.multiple_of(f * 32, 32), 32), :], sems)
    cholesky(m, l_ref, w_ref, lh, ll, vh, vl)
    lh[...], ll[...] = split(w_ref[...])
    inv = (lh[...], ll[...])
    both = jnp.concatenate([rhs_ref[...], cols_ref[...].T], 0)
    solved = mm(split(both), inv, 1, 1)
    y1_ref[...] = solved[:BLOCK]
    zx_ref[...] = mm(split(solved), inv)
    own = pos < PIVOTS // BLOCK

    @pl.when(own)
    def _():
        at = pl.ds(pl.multiple_of(pos * BLOCK, BLOCK), BLOCK)
        zx_ref[BLOCK:, :] = -w_ref[at, :]
        top_ref[...] = l_ref[:, at]

    @pl.when(jnp.logical_not(own))
    def _():
        top_ref[...] = jnp.zeros_like(top_ref)


def factor(pos, cols_top, rhs_top, bundles):
    return pl.pallas_call(
        factor_kernel,
        out_shape=(f32(PIVOTS, PIVOTS), f32(PIVOTS, BLOCK), f32(BLOCK, PIVOTS), f32(2 * BLOCK, PIVOTS)),
        in_specs=[SMEM, VMEM, VMEM] + [ANY] * 8,
        out_specs=(VMEM,) * 4,
        scratch_shapes=[pltpu.VMEM((PIVOTS, PIVOTS), jnp.float32)] * 2
        + [pltpu.VMEM((PIVOTS, PIVOTS), jnp.bfloat16)] * 2
        + [pltpu.VMEM((BLOCK, BLOCK), jnp.bfloat16)] * 2
        + [pltpu.SemaphoreType.DMA((32,))],
        compiler_params=pltpu.CompilerParams(vmem_limit_bytes=48 << 20),
        cost_estimate=pl.CostEstimate(flops=40 * 10**9, bytes_accessed=16 << 20, transcendentals=0),
        name="factor",
    )(pos, cols_top, rhs_top, *bundles)


CHIPS = SIDE * SIDE
FIRST = PIVOTS // (2 * BLOCK)
HALF = (CHIPS - FIRST) * BLOCK
WIDE = 512


def load_half(pos, bundles, held, sems):
    copies = []
    for e in range(SIDE):
        for d in range(SIDE):
            chip = place(pos, 0, e, d) // 2
            to = held.at[:, pl.ds(pl.multiple_of(chip * BLOCK, BLOCK), BLOCK)]
            copy = pltpu.make_async_copy(bundles[e].at[d], to, sems.at[e * SIDE + d])
            copy.start()
            copies.append(copy)
    for copy in copies:
        copy.wait()


HALF_SCRATCH = [pltpu.VMEM((PIVOTS, CHIPS * BLOCK), jnp.float32), pltpu.SemaphoreType.DMA((CHIPS,))]


def lanes(s, core):
    return pl.ds(pl.multiple_of(2 * BLOCK * s + BLOCK * core, BLOCK), BLOCK)


def ancestor_kernel(pos_ref, own_ref, par_ref, *refs):
    bundles, (mine_ref, other_ref, packed, held, sems) = refs[:4], refs[4:]
    pos = pos_ref[0]
    core = pos % 2
    for s in range(CHIPS - FIRST):
        packed[:BLOCK, BLOCK * s : BLOCK * (s + 1)] = own_ref[:, lanes(s, core)]
        packed[BLOCK:, BLOCK * s : BLOCK * (s + 1)] = par_ref[:, lanes(s, core)]
    load_half(pos, bundles, held, sems)
    total = None
    for n in range(0, HALF, WIDE):
        top = held[:, FIRST * BLOCK + n : FIRST * BLOCK + n + WIDE]
        term = mm(split(packed[:, n : n + WIDE]), split(top), 1, 1)
        total = term if total is None else total + term
    mine_ref[...] = total[:BLOCK]
    other_ref[...] = total[BLOCK:]


def ancestor(pos, own, par, bundles):
    return pl.pallas_call(
        ancestor_kernel,
        out_shape=(f32(BLOCK, PIVOTS),) * 2,
        in_specs=[SMEM, VMEM, VMEM] + [ANY] * 4,
        out_specs=(VMEM, VMEM),
        scratch_shapes=[pltpu.VMEM((2 * BLOCK, HALF), jnp.float32)] + HALF_SCRATCH,
        compiler_params=pltpu.CompilerParams(vmem_limit_bytes=40 << 20),
        cost_estimate=pl.CostEstimate(flops=3 * 10**9, bytes_accessed=12 << 20, transcendentals=0),
        name="ancestor",
    )(pos, own, par, *bundles)


def pivot_kernel(weight_ref, y1_ref, mine_ref, other_ref, w_ref, field_ref, terms_ref):
    inv = split(w_ref[...])
    inner = y1_ref[...] - mm(split(mine_ref[...] + other_ref[...]), inv, 1, 1)
    field = mm(split(inner), inv)
    field_ref[...] = field
    half = BLOCK // 2
    terms_ref[...] = weight_ref[0] * jnp.sum(field[:half] * field[half:], axis=0, keepdims=True)


def pivot(weight, y1, mine, other, w):
    return pl.pallas_call(
        pivot_kernel,
        out_shape=(f32(BLOCK, PIVOTS), f32(1, PIVOTS)),
        in_specs=[SMEM, VMEM, VMEM, VMEM, VMEM],
        out_specs=(VMEM, VMEM),
        compiler_params=pltpu.CompilerParams(vmem_limit_bytes=32 << 20),
        cost_estimate=pl.CostEstimate(flops=2 * 10**9, bytes_accessed=6 << 20, transcendentals=0),
        name="pivot",
    )(weight, y1, mine, other, w)


def update_kernel(pos_ref, own_ref, par_ref, *refs):
    bundles, (mine_ref, other_ref, held, sems) = refs[:4], refs[4:]
    load_half(pos_ref[0], bundles, held, sems)
    zx = split(jnp.concatenate([own_ref[...], par_ref[...]], 0))
    for n in range(0, HALF, WIDE):
        out = mm(zx, split(held[:, FIRST * BLOCK + n : FIRST * BLOCK + n + WIDE]))
        mine_ref[:, n : n + WIDE] = out[: 2 * BLOCK]
        other_ref[:, n : n + WIDE] = out[2 * BLOCK :]


def update(pos, own, par, bundles):
    return pl.pallas_call(
        update_kernel,
        out_shape=(f32(2 * BLOCK, HALF),) * 2,
        in_specs=[SMEM, VMEM, VMEM] + [ANY] * 4,
        out_specs=(VMEM, VMEM),
        scratch_shapes=HALF_SCRATCH,
        compiler_params=pltpu.CompilerParams(vmem_limit_bytes=40 << 20),
        cost_estimate=pl.CostEstimate(flops=5 * 10**9, bytes_accessed=12 << 20, transcendentals=0),
        name="update",
    )(pos, own, par, *bundles)


def finish_kernel(pos_ref, rest_ref, top_ref, rhs_ref, mine_ref, other_ref, front_ref, up_ref):
    pos = pos_ref[0]
    front_ref[:PIVOTS, :] = top_ref[...]
    own = pos < PIVOTS // BLOCK
    for s in range(CHIPS - FIRST):
        for side, ref in enumerate((mine_ref, other_ref)):
            out = ref[:, BLOCK * s : BLOCK * (s + 1)]
            at = lanes(s, (pos + side) % 2)
            up_ref[:, at] = rhs_ref[:, at] - out[:BLOCK]
            old = jnp.where(own, 0.0, rest_ref[at, :])
            down = pl.ds(pl.multiple_of(PIVOTS + 2 * BLOCK * s + BLOCK * ((pos + side) % 2), BLOCK), BLOCK)
            front_ref[down, :] = old - out[BLOCK:].T


def finish(pos, rest, top, rhs, mine, other):
    return pl.pallas_call(
        finish_kernel,
        out_shape=(f32(ORDER, BLOCK), f32(BLOCK, REST)),
        in_specs=[SMEM] + [VMEM] * 5,
        out_specs=(VMEM, VMEM),
        compiler_params=pltpu.CompilerParams(vmem_limit_bytes=32 << 20),
        cost_estimate=pl.CostEstimate(flops=10**9, bytes_accessed=12 << 20, transcendentals=0),
        name="finish",
    )(pos, rest, top, rhs, mine, other)


def axis_perm(shift, dy, dx):
    pairs = []
    for y in range(SIDE):
        for x in range(SIDE):
            for c in range(2):
                to = ((y + dy * shift) % SIDE) * 8 + ((x + dx * shift) % SIDE) * 2 + c
                pairs.append((y * 8 + x * 2 + c, to))
    return pairs


def ring_sum(v, sent):
    one, two, three = sent
    return (v + two) + (one + three)


def front_ring(v, dy, dx):
    return [send(v, axis_perm(s, dy, dx)) for s in (1, 2, 3)]


def damp_ring(v):
    return [lax.ppermute(v, "damp", [(i, (i + s) % 4) for i in range(4)]) for s in (1, 2, 3)]


tie = lax.optimization_barrier


def right_sides(src_index, src_amp, rec_index, resid, first, count):
    ids = jnp.arange(first, first + count, dtype=jnp.int32)
    forward = jnp.where(src_index[:, None] == ids[None, :], src_amp[:, None], 0.0)
    table = (rec_index[:, None] == ids[None, :]).astype(jnp.float32)
    adjoint = lax.dot_general(resid, table, (((0,), (0,)), ((), ())), precision=lax.Precision.HIGHEST)
    return jnp.concatenate([forward, adjoint], 0)


def per_device(
    base_front,
    child_blocks,
    child_map,
    src_index,
    src_amp,
    rec_index,
    rec_resid,
    ancestor_field,
    damp_weight,
):
    position = lax.axis_index("front")
    pos = position.reshape(1).astype(jnp.int32)
    base = base_front[0]
    maps = child_map[0]
    bundles = spread(pack(jnp.swapaxes(child_blocks[0], 1, 2)))
    base_t = base[:PIVOTS].T
    base_rows = 0.0
    for r in range(4):
        base_rows = base_rows + send(base_t[32 * r : 32 * r + 32], [(j, 4 * j + r) for j in range(8)])
    above = jnp.swapaxes(ancestor_field[0], 1, 2).reshape(BLOCK, REST)
    above_par = send(above, PARTNER)
    sides = (src_index, src_amp, rec_index, rec_resid[0])
    rhs_top = right_sides(*sides, 0, PIVOTS)
    rhs_rest = right_sides(*sides, PIVOTS, REST)
    bundles, base_rows, above_par, rhs_top, rhs_rest = tie((bundles, base_rows, above_par, rhs_top, rhs_rest))
    rows = pivot_rows(pos, maps, base_rows, bundles)
    bundles, rows = tie((bundles, rows))
    cols_top, cols_rest = columns(pos, maps, base, bundles)
    row_bundle = jnp.stack(ring(rows, 0))
    row_bundle, cols_top = tie((row_bundle, cols_top))
    row_own = ring(row_bundle, 1)
    row_bundles = row_own + [send(b, PARTNER) for b in row_own]
    top_bundle = jnp.stack(ring(cols_top, 0))
    row_bundles, top_bundle = tie((row_bundles, top_bundle))
    halves = ring(top_bundle, 1)
    w, top, y1, zx = factor(pos, cols_top, rhs_top, row_bundles)
    halves, w = tie((halves, w))
    zx_par = send(zx, PARTNER)
    mine, other = ancestor(pos, above, above_par, halves)
    field, terms = pivot(damp_weight, y1, mine, send(other, PARTNER), w)
    v = terms.reshape(8, BLOCK)
    v = v + send(v, PARTNER)
    v, zx = tie((v, zx))
    sent = front_ring(v, 0, 1)
    mine, other = update(pos, zx, zx_par, halves)
    v = ring_sum(v, sent)
    v, other = tie((v, other))
    sent = front_ring(v, 1, 0)
    other = send(other, PARTNER)
    v = ring_sum(v, sent)
    v, other = tie((v, other))
    sent = damp_ring(v)
    factored, up = finish(pos, cols_rest, top, rhs_rest, mine, other)
    summed = ring_sum(v, sent)
    gradient = lax.dynamic_slice_in_dim(summed.reshape(PIVOTS), position * 32, 32, 0)
    upward = jnp.swapaxes(up.reshape(2, BLOCK // 2, REST), 1, 2)
    pivot_field = jnp.swapaxes(field.reshape(2, BLOCK // 2, PIVOTS), 1, 2)
    return (factored[None], upward[None], pivot_field[None], gradient)


def solution(mesh):
    return jax.shard_map(
        per_device,
        mesh=mesh,
        in_specs=(
            P("damp", None, "front"),
            P("damp", None, None, "front"),
            P("damp", None, None),
            P("front"),
            P("front"),
            P(),
            P("damp", None, "front"),
            P("damp", None, None, "front"),
            P("damp"),
        ),
        out_specs=(
            P("damp", None, "front"),
            P("damp", None, None, "front"),
            P("damp", None, None, "front"),
            P("front"),
        ),
        check_vma=False,
    )
```

```python
import functools

import jax
import jax.numpy as jnp
from jax import lax
from jax.experimental import pallas as pl
from jax.experimental.pallas import tpu as pltpu
from jax.sharding import PartitionSpec as P

ORDER = 4096
PIVOTS = 1024
REST = ORDER - PIVOTS
BLOCK = 128
SIDE = 4


def split(a):
    hi = a.astype(jnp.bfloat16)
    lo = (a - hi.astype(jnp.float32)).astype(jnp.bfloat16)
    return hi, lo


def dg(a, b, ca, cb):
    return lax.dot_general(a, b, (((ca,), (cb,)), ((), ())), preferred_element_type=jnp.float32)


def mm(a, b, ca=1, cb=0):
    return dg(a[0], b[0], ca, cb) + (dg(a[0], b[1], ca, cb) + dg(a[1], b[0], ca, cb))


def front_perm(shift, along_x_core):
    pairs = []
    for y in range(SIDE):
        for x in range(SIDE):
            for c in range(2):
                dy, dx = (0, shift) if c == along_x_core else (shift, 0)
                to = ((y + dy) % SIDE) * 8 + ((x + dx) % SIDE) * 2 + c
                pairs.append((y * 8 + x * 2 + c, to))
    return pairs


PARTNER = [(i, i ^ 1) for i in range(32)]


def send(v, pairs):
    return lax.ppermute(v, "front", pairs)


def ring(v, along_x_core):
    back, two, on = (send(v, front_perm(s, along_x_core)) for s in (-1, 2, 1))
    return [v, back, two, on]


def spread(v):
    bundle = jnp.stack(ring(v, 0))
    own = ring(bundle, 1)
    return own + [send(b, PARTNER) for b in own]


def place(pos, which, e, d):
    core, x, y = pos % 2, (pos // 2) % SIDE, pos // 8
    if which:
        core = 1 - core
    first = core == 0
    yy = (y + jnp.where(first, e, d)) % SIDE
    xx = (x + jnp.where(first, d, e)) % SIDE
    return yy * 8 + xx * 2 + core


def fetch(pos, bundles, put):
    for which in range(2):
        for e in range(SIDE):
            for d in range(SIDE):
                put(place(pos, which, e, d), bundles[which * 4 + e].at[d])


ANY = pl.BlockSpec(memory_space=pltpu.HBM)
VMEM = pl.BlockSpec(memory_space=pltpu.VMEM)
SMEM = pl.BlockSpec(memory_space=pltpu.SMEM)


def f32(*shape):
    return jax.ShapeDtypeStruct(shape, jnp.float32)


PACKED = 5 * BLOCK


def pack(block):
    start = lax.axis_index("front") // 4 * BLOCK
    twice = jnp.concatenate([block, block[:, :, : PACKED - BLOCK]], 2)
    return lax.dynamic_slice_in_dim(twice, start, PACKED, 2)


def picked(map_row, rows, block):
    take = (map_row == rows).astype(jnp.bfloat16)
    panels = [take[:, BLOCK * i : BLOCK * (i + 1)] for i in range(8)]
    sums = [[None] * 8, [None] * 8]

    def put(part, j, term):
        old = sums[part][j]
        sums[part][j] = term if old is None else old + term

    for i in range(8):
        ahead = jnp.concatenate([panels[(i + t) % 8] for t in (1, 2, 3)], 1)
        for part, held in enumerate(split(block[BLOCK * i : BLOCK * (i + 1), :])):
            straight = dg(panels[i], held, 1, 0)
            for t in range(5):
                put(part, (i + t) % 8, straight[:, BLOCK * t : BLOCK * (t + 1)])
            put(part, i, dg(ahead, held[:, BLOCK : 4 * BLOCK], 1, 1))
    return tuple(jnp.concatenate(p, 1).astype(jnp.bfloat16) for p in sums)


def fetch_children(pos, bundles, blocks):
    def put(f, entry):
        blocks[:, pl.ds(pl.multiple_of(f * 32, 32), 32), :] = entry[...]

    fetch(pos, bundles, put)


CHILD_SCRATCH = [pltpu.VMEM((2, 1024, PACKED), jnp.float32)]


def tops_kernel(pos_ref, map_ref, base_ref, *refs):
    bundles, (top_ref, picks_ref, blocks) = refs[:8], refs[8:]
    pos = pos_ref[0]
    fetch_children(pos, bundles, blocks)
    top_ref[...] = base_ref[...]

    def child(c, _):
        map_row = map_ref[pl.ds(c, 1), :]
        few = lax.broadcasted_iota(jnp.int32, (32, 1024), 0) + pos * 32
        many = lax.broadcasted_iota(jnp.int32, (BLOCK, 1024), 0) + pos * BLOCK
        hi, lo = picked(map_row, jnp.concatenate([many, few], 0), blocks.at[c])
        picks = jnp.concatenate([hi[:BLOCK], lo[:BLOCK], hi[BLOCK:], lo[BLOCK:]], 0)
        picks_ref[pl.ds(c, 1)] = picks[None]
        where = (map_row == lax.broadcasted_iota(jnp.int32, (PIVOTS, 1024), 0)).astype(jnp.bfloat16)
        both = dg(where, picks[: 2 * BLOCK], 1, 1)
        top_ref[...] = top_ref[...] + (both[:, :BLOCK] + both[:, BLOCK:])
        return 0

    lax.fori_loop(0, 2, child, 0)


PICKS = 2 * (BLOCK + 32)


def assemble_tops(pos, maps, base_top, bundles):
    return pl.pallas_call(
        tops_kernel,
        out_shape=(f32(PIVOTS, BLOCK), jax.ShapeDtypeStruct((2, PICKS, 1024), jnp.bfloat16)),
        in_specs=[SMEM, VMEM, VMEM] + [VMEM] * 8,
        out_specs=(VMEM,) * 2,
        scratch_shapes=CHILD_SCRATCH,
        compiler_params=pltpu.CompilerParams(vmem_limit_bytes=32 << 20),
        cost_estimate=pl.CostEstimate(flops=4 * 10**9, bytes_accessed=8 << 20, transcendentals=0),
        name="assemble_tops",
    )(pos, maps, base_top, *bundles)


def pivot_rows_kernel(map_ref, base_ref, picks_ref, out_ref):
    out_ref[...] = base_ref[...]

    def child(c, _):
        rows = lax.broadcasted_iota(jnp.int32, (PIVOTS, 1024), 0)
        where = (map_ref[pl.ds(c, 1), :] == rows).astype(jnp.bfloat16)
        both = dg(picks_ref[pl.ds(c, 1), 2 * BLOCK :, :][0], where, 1, 1)
        out_ref[...] = out_ref[...] + (both[:32] + both[32:])
        return 0

    lax.fori_loop(0, 2, child, 0)


def pivot_rows(maps, base_rows, picks):
    return pl.pallas_call(
        pivot_rows_kernel,
        out_shape=f32(32, PIVOTS),
        in_specs=[VMEM] * 3,
        out_specs=VMEM,
        compiler_params=pltpu.CompilerParams(vmem_limit_bytes=16 << 20),
        cost_estimate=pl.CostEstimate(flops=10**9, bytes_accessed=2 << 20, transcendentals=0),
        name="pivot_rows",
    )(maps, base_rows, picks)


def rest_kernel(map_ref, base_ref, picks_ref, out_ref):
    tall = 512

    def chunk(i, _):
        at = pl.multiple_of(i * tall, tall)
        rows = lax.broadcasted_iota(jnp.int32, (tall, 1024), 0) + (at + PIVOTS)
        total = None
        for child in range(2):
            where = (map_ref[child : child + 1, :] == rows).astype(jnp.bfloat16)
            term = dg(where, picks_ref[child, : 2 * BLOCK, :], 1, 1)
            total = term if total is None else total + term
        out_ref[pl.ds(at, tall), :] = base_ref[pl.ds(at, tall), :] + (total[:, :BLOCK] + total[:, BLOCK:])
        return 0

    lax.fori_loop(0, REST // tall, chunk, 0)


def assemble_rest(maps, base_rest, picks):
    return pl.pallas_call(
        rest_kernel,
        out_shape=f32(REST, BLOCK),
        in_specs=[VMEM] * 3,
        out_specs=VMEM,
        compiler_params=pltpu.CompilerParams(vmem_limit_bytes=24 << 20),
        cost_estimate=pl.CostEstimate(flops=4 * 10**9, bytes_accessed=5 << 20, transcendentals=0),
        name="assemble_rest",
    )(maps, base_rest, picks)


def factor_block(block, spare):
    tiles = BLOCK // 8
    left = [block[8 * r : 8 * r + 8, :] for r in range(tiles)]
    upper = []
    lane = lax.broadcasted_iota(jnp.int32, (8, BLOCK), 1)
    sub = lax.broadcasted_iota(jnp.int32, (8, BLOCK), 0)

    def wide(x):
        return jnp.broadcast_to(x, (8, BLOCK))

    for top in range(tiles):
        first = 8 * top
        cols = [[wide(left[r][:, first + q : first + q + 1]) for r in range(top, tiles)] for q in range(8)]
        for q in range(8):
            spare[8 * q : 8 * q + 8, :] = cols[q][0]
        spare[64:72, :] = left[top]
        spare[72:80, :] = jnp.where(lane < first, left[top], jnp.where(lane == sub + first, 1.0, 0.0))
        low = {(i, q): wide(spare[8 * q + i : 8 * q + i + 1, :]) for i in range(8) for q in range(i + 1)}
        rows = [wide(spare[64 + q : 65 + q, :]) for q in range(8)]
        inv = [wide(spare[72 + q : 73 + q, :]) for q in range(8)]
        scale = []
        for q in range(8):
            scale.append(lax.rsqrt(low[q, q]))
            for i in range(q + 1, 8):
                low[i, q] = low[i, q] * scale[q]
            for i in range(q + 1, 8):
                for n in range(q + 1, i + 1):
                    low[i, n] = low[i, n] - low[i, q] * low[n, q]
        for q in range(8):
            for n in range(q):
                rows[q] = rows[q] - low[q, n] * rows[n]
                inv[q] = inv[q] - low[q, n] * inv[n]
            rows[q] = rows[q] * scale[q]
            inv[q] = inv[q] * scale[q]
        both = [jnp.where(lane < first + 8, inv[q], rows[q]) for q in range(8)]
        up, back = rows[0], inv[0]
        for q in range(1, 8):
            up = jnp.where(sub == q, rows[q], up)
            back = jnp.where(sub == q, inv[q], back)
        keep = (lane < first) | (lane >= first + 8)
        for r in range(top + 1, tiles):
            factors = []
            for q in range(8):
                t = cols[q][r - top]
                for n in range(q):
                    t = t - factors[n] * low[q, n]
                factors.append(t * scale[q])
            t = jnp.where(keep, left[r], 0.0)
            for q in range(8):
                t = t - factors[q] * both[q]
            left[r] = t
        upper.append(up)
        left[top] = back
    return jnp.concatenate(upper, 0), jnp.concatenate(left, 0)


def cholesky(m, l_ref, w_ref, lh, ll, vh, vl, spare):
    w_ref[...] = jnp.zeros_like(w_ref)
    l_ref[...] = jnp.zeros_like(l_ref)
    row = lax.broadcasted_iota(jnp.int32, (BLOCK, BLOCK), 0)
    col = lax.broadcasted_iota(jnp.int32, (BLOCK, BLOCK), 1)
    panels = PIVOTS // BLOCK

    def step(k, _):
        at = pl.ds(pl.multiple_of(k * BLOCK, BLOCK), BLOCK)
        upper, inv = factor_block(m[at, at], spare)
        inv = jnp.where(row >= col, inv, 0.0)
        l_ref[at, at] = jnp.where(row >= col, upper.T, 0.0)
        w_ref[at, at] = inv
        vh[...], vl[...] = split(inv)
        for kk in range(panels - 1):

            @pl.when(k == kk)
            def _():
                a, b = kk * BLOCK, (kk + 1) * BLOCK
                below = mm(split(m[b:, a:b]), (vh[...], vl[...]), 1, 1)
                l_ref[b:, a:b] = below
                lh[b:, a:b], ll[b:, a:b] = split(below)
                ahead = slice(b, b + BLOCK)
                m[b:, ahead] = m[b:, ahead] - mm((lh[b:, :b], ll[b:, :b]), (lh[ahead, :b], ll[ahead, :b]), 1, 1)

        return 0

    lax.fori_loop(0, panels, step, 0)
    for s in (128, 256, 512):
        for a in range(0, PIVOTS, 2 * s):
            up, dn = slice(a, a + s), slice(a + s, a + 2 * s)
            inner = mm((lh[dn, up], ll[dn, up]), split(w_ref[up, up]))
            w_ref[dn, up] = -mm(split(w_ref[dn, dn]), split(inner))


def factor_kernel(pos_ref, cols_ref, rhs_ref, *refs):
    bundles, (w_ref, top_ref, y1_ref, zx_ref, m, l_ref, lh, ll, vh, vl, spare) = refs[:8], refs[8:]
    pos = pos_ref[0]

    def put(f, entry):
        m[pl.ds(pl.multiple_of(f * 32, 32), 32), :] = entry[...]

    fetch(pos, bundles, put)
    cholesky(m, l_ref, w_ref, lh, ll, vh, vl, spare)
    lh[...], ll[...] = split(w_ref[...])
    m[:BLOCK, :] = rhs_ref[...]
    m[BLOCK : 2 * BLOCK, :] = cols_ref[...].T
    both = split(m[: 2 * BLOCK, :])

    def down(n, _):
        at = pl.ds(pl.multiple_of(n * 256, 256), 256)
        m[2 * BLOCK : 4 * BLOCK, at] = mm(both, (lh[at, :], ll[at, :]), 1, 1)
        return 0

    lax.fori_loop(0, PIVOTS // 256, down, 0)
    y1_ref[...] = m[2 * BLOCK : 3 * BLOCK, :]
    solved = split(m[2 * BLOCK : 4 * BLOCK, :])

    def back(n, _):
        at = pl.ds(pl.multiple_of(n * 256, 256), 256)
        zx_ref[:, at] = mm(solved, (lh[:, at], ll[:, at]))
        return 0

    lax.fori_loop(0, PIVOTS // 256, back, 0)
    own = pos < PIVOTS // BLOCK

    @pl.when(own)
    def _():
        at = pl.ds(pl.multiple_of(pos * BLOCK, BLOCK), BLOCK)
        zx_ref[BLOCK:, :] = -w_ref[at, :]
        top_ref[...] = l_ref[:, at]

    @pl.when(jnp.logical_not(own))
    def _():
        top_ref[...] = jnp.zeros_like(top_ref)


def factor(pos, cols_top, rhs_top, bundles):
    return pl.pallas_call(
        factor_kernel,
        out_shape=(f32(PIVOTS, PIVOTS), f32(PIVOTS, BLOCK), f32(BLOCK, PIVOTS), f32(2 * BLOCK, PIVOTS)),
        in_specs=[SMEM, VMEM, VMEM] + [VMEM] * 8,
        out_specs=(VMEM,) * 4,
        scratch_shapes=[pltpu.VMEM((PIVOTS, PIVOTS), jnp.float32)] * 2
        + [pltpu.VMEM((PIVOTS, PIVOTS), jnp.bfloat16)] * 2
        + [pltpu.VMEM((BLOCK, BLOCK), jnp.bfloat16)] * 2
        + [pltpu.VMEM((80, BLOCK), jnp.float32)],
        compiler_params=pltpu.CompilerParams(vmem_limit_bytes=48 << 20),
        cost_estimate=pl.CostEstimate(flops=40 * 10**9, bytes_accessed=16 << 20, transcendentals=0),
        name="factor",
    )(pos, cols_top, rhs_top, *bundles)


CHIPS = SIDE * SIDE
FIRST = PIVOTS // (2 * BLOCK)
HALF = (CHIPS - FIRST) * BLOCK
WIDE = 512


def half_copies(pos, bundles, held, sems):
    for e in range(SIDE):
        for d in range(SIDE):
            chip = place(pos, 0, e, d) // 2
            to = held.at[:, pl.ds(pl.multiple_of(chip * BLOCK, BLOCK), BLOCK)]
            pltpu.make_async_copy(bundles[e].at[d], to, sems.at[chip]).start()


def half_wait(bundles, held, sems, chip):
    to = held.at[:, pl.ds(pl.multiple_of(chip * BLOCK, BLOCK), BLOCK)]
    pltpu.make_async_copy(bundles[0].at[0], to, sems.at[chip]).wait()


HALF_SCRATCH = [pltpu.VMEM((PIVOTS, CHIPS * BLOCK), jnp.float32), pltpu.SemaphoreType.DMA((CHIPS,))]


def lanes(s, core):
    return pl.ds(pl.multiple_of(2 * BLOCK * s + BLOCK * core, BLOCK), BLOCK)


def ancestor_kernel(pos_ref, own_ref, par_ref, *refs):
    bundles, (mine_ref, other_ref, packed, total, held, sems, more) = refs[:4], refs[4:]
    pos = pos_ref[0]
    core = pos % 2
    copies = []
    for s in range(CHIPS - FIRST):
        for side, ref in enumerate((own_ref, par_ref)):
            to = packed.at[BLOCK * side : BLOCK * (side + 1), BLOCK * s : BLOCK * (s + 1)]
            copies.append(pltpu.make_async_copy(ref.at[:, lanes(s, core)], to, more.at[2 * s + side]))
            copies[-1].start()
    half_copies(pos, bundles, held, sems)
    for chip in range(FIRST):
        half_wait(bundles, held, sems, chip)
    for copy in copies:
        copy.wait()
    total[...] = jnp.zeros_like(total)

    def chunk(n, _):
        for t in range(WIDE // BLOCK):
            half_wait(bundles, held, sems, FIRST + n * (WIDE // BLOCK) + t)
        at = pl.ds(pl.multiple_of(n * WIDE, WIDE), WIDE)
        there = pl.ds(pl.multiple_of(FIRST * BLOCK + n * WIDE, WIDE), WIDE)
        total[...] = total[...] + mm(split(packed[:, at]), split(held[:, there]), 1, 1)
        return 0

    lax.fori_loop(0, HALF // WIDE, chunk, 0)
    mine_ref[...] = total[:BLOCK, :]
    other_ref[...] = total[BLOCK:, :]


def ancestor(pos, own, par, bundles):
    return pl.pallas_call(
        ancestor_kernel,
        out_shape=(f32(BLOCK, PIVOTS),) * 2,
        in_specs=[SMEM] + [ANY] * 6,
        out_specs=(VMEM, VMEM),
        scratch_shapes=[pltpu.VMEM((2 * BLOCK, HALF), jnp.float32), pltpu.VMEM((2 * BLOCK, PIVOTS), jnp.float32)]
        + HALF_SCRATCH
        + [pltpu.SemaphoreType.DMA((2 * (CHIPS - FIRST),))],
        compiler_params=pltpu.CompilerParams(vmem_limit_bytes=32 << 20),
        cost_estimate=pl.CostEstimate(flops=3 * 10**9, bytes_accessed=12 << 20, transcendentals=0),
        name="ancestor",
    )(pos, own, par, *bundles)


def pivot_kernel(weight_ref, y1_ref, mine_ref, other_ref, w_ref, field_ref, terms_ref):
    inv = split(w_ref[...])
    inner = y1_ref[...] - mm(split(mine_ref[...] + other_ref[...]), inv, 1, 1)
    field = mm(split(inner), inv)
    field_ref[...] = field
    half = BLOCK // 2
    terms_ref[...] = weight_ref[0] * jnp.sum(field[:half] * field[half:], axis=0, keepdims=True)


def pivot(weight, y1, mine, other, w):
    return pl.pallas_call(
        pivot_kernel,
        out_shape=(f32(BLOCK, PIVOTS), f32(1, PIVOTS)),
        in_specs=[SMEM, VMEM, VMEM, VMEM, VMEM],
        out_specs=(VMEM, VMEM),
        compiler_params=pltpu.CompilerParams(vmem_limit_bytes=32 << 20),
        cost_estimate=pl.CostEstimate(flops=2 * 10**9, bytes_accessed=6 << 20, transcendentals=0),
        name="pivot",
    )(weight, y1, mine, other, w)


def update_kernel(pos_ref, first_ref, own_ref, par_ref, *refs):
    bundles, (mine_ref, other_ref, held, sems) = refs[:4], refs[4:]
    pos = pos_ref[0]
    low = first_ref[0]
    per = WIDE // BLOCK
    zx = split(jnp.concatenate([own_ref[...], par_ref[...]], 0))

    def each(act):
        for e in range(SIDE):
            for d in range(SIDE):
                slot = place(pos, 0, e, d) // 2 - low

                @pl.when((slot >= 0) & (slot < per))
                def _():
                    to = held.at[:, pl.ds(pl.multiple_of(slot * BLOCK, BLOCK), BLOCK)]
                    act(pltpu.make_async_copy(bundles[e].at[d], to, sems.at[e * SIDE + d]))

    each(lambda copy: copy.start())
    each(lambda copy: copy.wait())

    def chunk(n, _):
        at = pl.ds(pl.multiple_of(n * 256, 256), 256)
        out = mm(zx, split(held[:, at]))
        mine_ref[:, at] = out[: 2 * BLOCK]
        other_ref[:, at] = out[2 * BLOCK :]
        return 0

    lax.fori_loop(0, WIDE // 256, chunk, 0)


def update(pos, part, own, par, bundles):
    first = jnp.full((1,), FIRST + part * (WIDE // BLOCK), jnp.int32)
    return pl.pallas_call(
        update_kernel,
        out_shape=(f32(2 * BLOCK, WIDE),) * 2,
        in_specs=[SMEM, SMEM, VMEM, VMEM] + [ANY] * 4,
        out_specs=(VMEM, VMEM),
        scratch_shapes=[pltpu.VMEM((PIVOTS, WIDE), jnp.float32), pltpu.SemaphoreType.DMA((CHIPS,))],
        compiler_params=pltpu.CompilerParams(vmem_limit_bytes=20 << 20),
        cost_estimate=pl.CostEstimate(flops=2 * 10**9, bytes_accessed=5 << 20, transcendentals=0),
        name="update",
    )(pos, first, own, par, *bundles)


PARTS = HALF // WIDE


def finish_kernel(pos_ref, old_ref, *refs):
    updates, out_ref = refs[:-1], refs[-1]
    pos = pos_ref[0]
    for side in range(2):
        for part in range(PARTS):
            for t in range(WIDE // BLOCK):
                at = lanes(part * (WIDE // BLOCK) + t, (pos + side) % 2)
                out = updates[side * PARTS + part][:BLOCK, BLOCK * t : BLOCK * (t + 1)]
                out_ref[:, at] = old_ref[:, at] - out


def front_kernel(pos_ref, top_ref, old_ref, *refs):
    updates, out_ref = refs[:-1], refs[-1]
    pos = pos_ref[0]
    out_ref[:PIVOTS, :] = top_ref[...]
    own = pos < PIVOTS // BLOCK
    for side in range(2):
        core = (pos + side) % 2
        for part in range(PARTS):
            for t in range(WIDE // BLOCK):
                s = part * (WIDE // BLOCK) + t
                out = updates[side * PARTS + part][BLOCK:, BLOCK * t : BLOCK * (t + 1)]
                old = jnp.where(own, 0.0, old_ref[lanes(s, core), :])
                down = pl.ds(pl.multiple_of(PIVOTS + 2 * BLOCK * s + BLOCK * core, BLOCK), BLOCK)
                out_ref[down, :] = old - out.T


def finish(pos, rhs, updates):
    return pl.pallas_call(
        finish_kernel,
        out_shape=f32(BLOCK, REST),
        in_specs=[SMEM] + [VMEM] * (1 + len(updates)),
        out_specs=VMEM,
        compiler_params=pltpu.CompilerParams(vmem_limit_bytes=16 << 20),
        cost_estimate=pl.CostEstimate(flops=10**8, bytes_accessed=6 << 20, transcendentals=0),
        name="finish",
    )(pos, rhs, *updates)


def front(pos, top, rest, updates):
    return pl.pallas_call(
        front_kernel,
        out_shape=f32(ORDER, BLOCK),
        in_specs=[SMEM] + [VMEM] * (2 + len(updates)),
        out_specs=VMEM,
        compiler_params=pltpu.CompilerParams(vmem_limit_bytes=16 << 20),
        cost_estimate=pl.CostEstimate(flops=10**8, bytes_accessed=7 << 20, transcendentals=0),
        name="front",
    )(pos, top, rest, *updates)


PAIRS = ((1, 0, 3, 2), (3, 2, 1, 0))


def x_pairs(step):
    return [(i, i // 8 * 8 + PAIRS[step][i // 2 % SIDE] * 2 + i % 2) for i in range(32)]


def y_pairs(step):
    return [(i, PAIRS[step][i // 8] * 8 + i % 8) for i in range(32)]


def damp_pairs(step):
    return list(enumerate(PAIRS[step]))


tie = lax.optimization_barrier


def in_hbm(v):
    return pltpu.with_memory_space_constraint(v, pltpu.HBM)


def right_sides(src_index, src_amp, rec_index, resid, first, count):
    ids = jnp.arange(first, first + count, dtype=jnp.int32)
    forward = jnp.where(src_index[:, None] == ids[None, :], src_amp[:, None], 0.0)
    table = (rec_index[:, None] == ids[None, :]).astype(jnp.float32)
    adjoint = lax.dot_general(resid, table, (((0,), (0,)), ((), ())), precision=lax.Precision.HIGHEST)
    return jnp.concatenate([forward, adjoint], 0)


def per_device(
    base_front,
    child_blocks,
    child_map,
    src_index,
    src_amp,
    rec_index,
    rec_resid,
    ancestor_field,
    damp_weight,
):
    position = lax.axis_index("front")
    pos = position.reshape(1).astype(jnp.int32)
    base = base_front[0]
    maps = child_map[0]
    bundles = spread(pack(jnp.swapaxes(child_blocks[0], 1, 2)))
    base_t = base[:PIVOTS].T
    base_rows = 0.0
    for r in range(4):
        base_rows = base_rows + send(base_t[32 * r : 32 * r + 32], [(j, 4 * j + r) for j in range(8)])
    above = jnp.swapaxes(ancestor_field[0], 1, 2).reshape(BLOCK, REST)
    above_par = send(above, PARTNER)
    sides = (src_index, src_amp, rec_index, rec_resid[0])
    rhs_top = right_sides(*sides, 0, PIVOTS)
    rhs_rest = right_sides(*sides, PIVOTS, REST)
    base_top, base_rest = base[:PIVOTS], base[PIVOTS:]
    bundles, base_rows, above_par, rhs_top, rhs_rest = tie((bundles, base_rows, above_par, rhs_top, rhs_rest))
    cols_top, picks = assemble_tops(pos, maps, base_top, bundles)
    top_bundle = jnp.stack(ring(cols_top, 0))
    rows = pivot_rows(maps, base_rows, picks)
    rows, picks = tie((rows, picks))
    row_bundle = jnp.stack(ring(rows, 0))
    cols_rest = assemble_rest(maps, base_rest, picks)
    row_bundle, cols_rest, top_bundle = tie((row_bundle, cols_rest, top_bundle))
    row_own = ring(row_bundle, 1)
    row_own, top_bundle = tie((row_own, top_bundle))
    row_bundles = row_own + [send(b, PARTNER) for b in row_own]
    halves = ring(top_bundle, 1)
    w, top, y1, zx = factor(pos, cols_top, rhs_top, row_bundles)
    halves, w, zx = tie((halves, w, zx))
    zx_par = send(zx, PARTNER)
    mine, other = ancestor(pos, in_hbm(above), in_hbm(above_par), halves)
    field, terms = pivot(damp_weight, y1, mine, send(other, PARTNER), w)
    v = terms.reshape(8, BLOCK)
    v = v + send(v, PARTNER)
    mine, other = [], []

    def window(v, pairs, part):
        nonlocal zx
        v, zx = tie((v, zx))
        come = send(v, pairs)
        own, par = update(pos, part, zx, zx_par, halves)
        come, own, par = tie((come, own, par))
        mine.append(own)
        other.append(send(par, PARTNER))
        return v + come

    v = window(v, x_pairs(0), 0)
    v = window(v, x_pairs(1), 1)
    v = window(v, y_pairs(0), 2)
    v = v + send(v, y_pairs(1))
    updates = mine + other
    v, updates = tie((v, updates))
    come = lax.ppermute(v, "damp", damp_pairs(0))
    up = finish(pos, rhs_rest, updates)
    come, up = tie((come, up))
    v = v + come
    v, updates = tie((v, updates))
    come = lax.ppermute(v, "damp", damp_pairs(1))
    factored = front(pos, top, cols_rest, updates)
    summed = v + come
    gradient = lax.dynamic_slice_in_dim(summed.reshape(PIVOTS), position * 32, 32, 0)
    upward = jnp.swapaxes(up.reshape(2, BLOCK // 2, REST), 1, 2)
    pivot_field = jnp.swapaxes(field.reshape(2, BLOCK // 2, PIVOTS), 1, 2)
    return (factored[None], upward[None], pivot_field[None], gradient)


def solution(mesh):
    return jax.shard_map(
        per_device,
        mesh=mesh,
        in_specs=(
            P("damp", None, "front"),
            P("damp", None, None, "front"),
            P("damp", None, None),
            P("front"),
            P("front"),
            P(),
            P("damp", None, "front"),
            P("damp", None, None, "front"),
            P("damp"),
        ),
        out_specs=(
            P("damp", None, "front"),
            P("damp", None, None, "front"),
            P("damp", None, None, "front"),
            P("front"),
        ),
        check_vma=False,
    )
```

```python
import functools

import jax
import jax.numpy as jnp
from jax import lax
from jax.experimental import pallas as pl
from jax.experimental.pallas import tpu as pltpu
from jax.sharding import PartitionSpec as P

ORDER = 4096
PIVOTS = 1024
REST = ORDER - PIVOTS
BLOCK = 128
SIDE = 4


def split(a):
    hi = a.astype(jnp.bfloat16)
    lo = (a - hi.astype(jnp.float32)).astype(jnp.bfloat16)
    return hi, lo


def dg(a, b, ca, cb):
    return lax.dot_general(a, b, (((ca,), (cb,)), ((), ())), preferred_element_type=jnp.float32)


def mm(a, b, ca=1, cb=0):
    return dg(a[0], b[0], ca, cb) + (dg(a[0], b[1], ca, cb) + dg(a[1], b[0], ca, cb))


def front_perm(shift, along_x_core):
    pairs = []
    for y in range(SIDE):
        for x in range(SIDE):
            for c in range(2):
                dy, dx = (0, shift) if c == along_x_core else (shift, 0)
                to = ((y + dy) % SIDE) * 8 + ((x + dx) % SIDE) * 2 + c
                pairs.append((y * 8 + x * 2 + c, to))
    return pairs


PARTNER = [(i, i ^ 1) for i in range(32)]


def send(v, pairs):
    return lax.ppermute(v, "front", pairs)


def ring(v, along_x_core):
    back, two, on = (send(v, front_perm(s, along_x_core)) for s in (-1, 2, 1))
    return [v, back, two, on]


def spread(v):
    bundle = jnp.stack(ring(v, 0))
    own = ring(bundle, 1)
    return own + [send(b, PARTNER) for b in own]


def place(pos, which, e, d):
    core, x, y = pos % 2, (pos // 2) % SIDE, pos // 8
    if which:
        core = 1 - core
    first = core == 0
    yy = (y + jnp.where(first, e, d)) % SIDE
    xx = (x + jnp.where(first, d, e)) % SIDE
    return yy * 8 + xx * 2 + core


def fetch(pos, bundles, put):
    for which in range(2):
        for e in range(SIDE):
            for d in range(SIDE):
                put(place(pos, which, e, d), bundles[which * 4 + e].at[d])


ANY = pl.BlockSpec(memory_space=pltpu.HBM)
VMEM = pl.BlockSpec(memory_space=pltpu.VMEM)
SMEM = pl.BlockSpec(memory_space=pltpu.SMEM)


def f32(*shape):
    return jax.ShapeDtypeStruct(shape, jnp.float32)


PACKED = 5 * BLOCK


def pack(block):
    start = lax.axis_index("front") // 4 * BLOCK
    twice = jnp.concatenate([block, block[:, :, : PACKED - BLOCK]], 2)
    return lax.dynamic_slice_in_dim(twice, start, PACKED, 2)


def picked(map_row, rows, block):
    take = (map_row == rows).astype(jnp.bfloat16)
    panels = [take[:, BLOCK * i : BLOCK * (i + 1)] for i in range(8)]
    sums = [[None] * 8, [None] * 8]

    def put(part, j, term):
        old = sums[part][j]
        sums[part][j] = term if old is None else old + term

    for i in range(8):
        ahead = jnp.concatenate([panels[(i + t) % 8] for t in (1, 2, 3)], 1)
        for part, held in enumerate(split(block[BLOCK * i : BLOCK * (i + 1), :])):
            straight = dg(panels[i], held, 1, 0)
            for t in range(5):
                put(part, (i + t) % 8, straight[:, BLOCK * t : BLOCK * (t + 1)])
            put(part, i, dg(ahead, held[:, BLOCK : 4 * BLOCK], 1, 1))
    return tuple(jnp.concatenate(p, 1).astype(jnp.bfloat16) for p in sums)


def fetch_children(pos, bundles, blocks):
    def put(f, entry):
        blocks[:, pl.ds(pl.multiple_of(f * 32, 32), 32), :] = entry[...]

    fetch(pos, bundles, put)


CHILD_SCRATCH = [pltpu.VMEM((2, 1024, PACKED), jnp.float32)]


def tops_kernel(pos_ref, map_ref, base_ref, *refs):
    bundles, (top_ref, picks_ref, blocks) = refs[:8], refs[8:]
    pos = pos_ref[0]
    fetch_children(pos, bundles, blocks)
    top_ref[...] = base_ref[...]

    def child(c, _):
        map_row = map_ref[pl.ds(c, 1), :]
        few = lax.broadcasted_iota(jnp.int32, (32, 1024), 0) + pos * 32
        many = lax.broadcasted_iota(jnp.int32, (BLOCK, 1024), 0) + pos * BLOCK
        hi, lo = picked(map_row, jnp.concatenate([many, few], 0), blocks.at[c])
        picks = jnp.concatenate([hi[:BLOCK], lo[:BLOCK], hi[BLOCK:], lo[BLOCK:]], 0)
        picks_ref[pl.ds(c, 1)] = picks[None]
        where = (map_row == lax.broadcasted_iota(jnp.int32, (PIVOTS, 1024), 0)).astype(jnp.bfloat16)
        both = dg(where, picks[: 2 * BLOCK], 1, 1)
        top_ref[...] = top_ref[...] + (both[:, :BLOCK] + both[:, BLOCK:])
        return 0

    lax.fori_loop(0, 2, child, 0)


PICKS = 2 * (BLOCK + 32)


def assemble_tops(pos, maps, base_top, bundles):
    return pl.pallas_call(
        tops_kernel,
        out_shape=(f32(PIVOTS, BLOCK), jax.ShapeDtypeStruct((2, PICKS, 1024), jnp.bfloat16)),
        in_specs=[SMEM, VMEM, VMEM] + [VMEM] * 8,
        out_specs=(VMEM,) * 2,
        scratch_shapes=CHILD_SCRATCH,
        compiler_params=pltpu.CompilerParams(vmem_limit_bytes=32 << 20),
        cost_estimate=pl.CostEstimate(flops=4 * 10**9, bytes_accessed=8 << 20, transcendentals=0),
        name="assemble_tops",
    )(pos, maps, base_top, *bundles)


def pivot_rows_kernel(map_ref, base_ref, picks_ref, out_ref):
    out_ref[...] = base_ref[...]

    def child(c, _):
        rows = lax.broadcasted_iota(jnp.int32, (PIVOTS, 1024), 0)
        where = (map_ref[pl.ds(c, 1), :] == rows).astype(jnp.bfloat16)
        both = dg(picks_ref[pl.ds(c, 1), 2 * BLOCK :, :][0], where, 1, 1)
        out_ref[...] = out_ref[...] + (both[:32] + both[32:])
        return 0

    lax.fori_loop(0, 2, child, 0)


def pivot_rows(maps, base_rows, picks):
    return pl.pallas_call(
        pivot_rows_kernel,
        out_shape=f32(32, PIVOTS),
        in_specs=[VMEM] * 3,
        out_specs=VMEM,
        compiler_params=pltpu.CompilerParams(vmem_limit_bytes=16 << 20),
        cost_estimate=pl.CostEstimate(flops=10**9, bytes_accessed=2 << 20, transcendentals=0),
        name="pivot_rows",
    )(maps, base_rows, picks)


def rest_kernel(map_ref, base_ref, picks_ref, out_ref):
    tall = 512

    def chunk(i, _):
        at = pl.multiple_of(i * tall, tall)
        rows = lax.broadcasted_iota(jnp.int32, (tall, 1024), 0) + (at + PIVOTS)
        total = None
        for child in range(2):
            where = (map_ref[child : child + 1, :] == rows).astype(jnp.bfloat16)
            term = dg(where, picks_ref[child, : 2 * BLOCK, :], 1, 1)
            total = term if total is None else total + term
        out_ref[pl.ds(at, tall), :] = base_ref[pl.ds(at, tall), :] + (total[:, :BLOCK] + total[:, BLOCK:])
        return 0

    lax.fori_loop(0, REST // tall, chunk, 0)


def assemble_rest(maps, base_rest, picks):
    return pl.pallas_call(
        rest_kernel,
        out_shape=f32(REST, BLOCK),
        in_specs=[VMEM] * 3,
        out_specs=VMEM,
        compiler_params=pltpu.CompilerParams(vmem_limit_bytes=24 << 20),
        cost_estimate=pl.CostEstimate(flops=4 * 10**9, bytes_accessed=5 << 20, transcendentals=0),
        name="assemble_rest",
    )(maps, base_rest, picks)


def factor_block(block, spare):
    tiles = BLOCK // 8
    left = [block[8 * r : 8 * r + 8, :] for r in range(tiles)]
    upper = []
    lane = lax.broadcasted_iota(jnp.int32, (8, BLOCK), 1)
    sub = lax.broadcasted_iota(jnp.int32, (8, BLOCK), 0)

    def wide(x):
        return jnp.broadcast_to(x, (8, BLOCK))

    for top in range(tiles):
        first = 8 * top
        cols = [[wide(left[r][:, first + q : first + q + 1]) for r in range(top, tiles)] for q in range(8)]
        for q in range(8):
            spare[8 * q : 8 * q + 8, :] = cols[q][0]
        spare[64:72, :] = left[top]
        spare[72:80, :] = jnp.where(lane < first, left[top], jnp.where(lane == sub + first, 1.0, 0.0))
        low = {(i, q): wide(spare[8 * q + i : 8 * q + i + 1, :]) for i in range(8) for q in range(i + 1)}
        rows = [wide(spare[64 + q : 65 + q, :]) for q in range(8)]
        inv = [wide(spare[72 + q : 73 + q, :]) for q in range(8)]
        scale = []
        for q in range(8):
            scale.append(lax.rsqrt(low[q, q]))
            for i in range(q + 1, 8):
                low[i, q] = low[i, q] * scale[q]
            for i in range(q + 1, 8):
                for n in range(q + 1, i + 1):
                    low[i, n] = low[i, n] - low[i, q] * low[n, q]
        for q in range(8):
            for n in range(q):
                rows[q] = rows[q] - low[q, n] * rows[n]
                inv[q] = inv[q] - low[q, n] * inv[n]
            rows[q] = rows[q] * scale[q]
            inv[q] = inv[q] * scale[q]
        both = [jnp.where(lane < first + 8, inv[q], rows[q]) for q in range(8)]
        up, back = rows[0], inv[0]
        for q in range(1, 8):
            up = jnp.where(sub == q, rows[q], up)
            back = jnp.where(sub == q, inv[q], back)
        keep = (lane < first) | (lane >= first + 8)
        for r in range(top + 1, tiles):
            factors = []
            for q in range(8):
                t = cols[q][r - top]
                for n in range(q):
                    t = t - factors[n] * low[q, n]
                factors.append(t * scale[q])
            t = jnp.where(keep, left[r], 0.0)
            for q in range(8):
                t = t - factors[q] * both[q]
            left[r] = t
        upper.append(up)
        left[top] = back
    return jnp.concatenate(upper, 0), jnp.concatenate(left, 0)


def cholesky(m, l_ref, w_ref, lh, ll, vh, vl, spare):
    w_ref[...] = jnp.zeros_like(w_ref)
    l_ref[...] = jnp.zeros_like(l_ref)
    row = lax.broadcasted_iota(jnp.int32, (BLOCK, BLOCK), 0)
    col = lax.broadcasted_iota(jnp.int32, (BLOCK, BLOCK), 1)
    panels = PIVOTS // BLOCK

    def step(k, _):
        at = pl.ds(pl.multiple_of(k * BLOCK, BLOCK), BLOCK)
        upper, inv = factor_block(m[at, at], spare)
        inv = jnp.where(row >= col, inv, 0.0)
        l_ref[at, at] = jnp.where(row >= col, upper.T, 0.0)
        w_ref[at, at] = inv
        vh[...], vl[...] = split(inv)
        for kk in range(panels - 1):

            @pl.when(k == kk)
            def _():
                a, b = kk * BLOCK, (kk + 1) * BLOCK
                below = mm(split(m[b:, a:b]), (vh[...], vl[...]), 1, 1)
                l_ref[b:, a:b] = below
                lh[b:, a:b], ll[b:, a:b] = split(below)
                ahead = slice(b, b + BLOCK)
                m[b:, ahead] = m[b:, ahead] - mm((lh[b:, :b], ll[b:, :b]), (lh[ahead, :b], ll[ahead, :b]), 1, 1)

        return 0

    lax.fori_loop(0, panels, step, 0)
    for s in (128, 256, 512):
        for a in range(0, PIVOTS, 2 * s):
            up, dn = slice(a, a + s), slice(a + s, a + 2 * s)
            inner = mm((lh[dn, up], ll[dn, up]), split(w_ref[up, up]))
            w_ref[dn, up] = -mm(split(w_ref[dn, dn]), split(inner))


def collect_kernel(pos_ref, *refs):
    bundles, out_ref = refs[:8], refs[8]

    def put(f, entry):
        out_ref[pl.ds(pl.multiple_of(f * 32, 32), 32), :] = entry[...]

    fetch(pos_ref[0], bundles, put)


def collect(pos, bundles):
    return pl.pallas_call(
        collect_kernel,
        out_shape=f32(PIVOTS, PIVOTS),
        in_specs=[SMEM] + [VMEM] * 8,
        out_specs=VMEM,
        compiler_params=pltpu.CompilerParams(vmem_limit_bytes=16 << 20),
        cost_estimate=pl.CostEstimate(flops=0, bytes_accessed=8 << 20, transcendentals=0),
        name="collect",
    )(pos, *bundles)


def factor_kernel(pos_ref, cols_ref, rhs_ref, block_ref, *refs):
    w_ref, top_ref, y1_ref, zx_ref, m, l_ref, lh, ll, vh, vl, spare = refs
    pos = pos_ref[0]
    m[...] = block_ref[...]
    cholesky(m, l_ref, w_ref, lh, ll, vh, vl, spare)
    lh[...], ll[...] = split(w_ref[...])
    m[:BLOCK, :] = rhs_ref[...]
    m[BLOCK : 2 * BLOCK, :] = cols_ref[...].T
    both = split(m[: 2 * BLOCK, :])

    def down(n, _):
        at = pl.ds(pl.multiple_of(n * 256, 256), 256)
        m[2 * BLOCK : 4 * BLOCK, at] = mm(both, (lh[at, :], ll[at, :]), 1, 1)
        return 0

    lax.fori_loop(0, PIVOTS // 256, down, 0)
    y1_ref[...] = m[2 * BLOCK : 3 * BLOCK, :]
    solved = split(m[2 * BLOCK : 4 * BLOCK, :])

    def back(n, _):
        at = pl.ds(pl.multiple_of(n * 256, 256), 256)
        zx_ref[:, at] = mm(solved, (lh[:, at], ll[:, at]))
        return 0

    lax.fori_loop(0, PIVOTS // 256, back, 0)
    own = pos < PIVOTS // BLOCK

    @pl.when(own)
    def _():
        at = pl.ds(pl.multiple_of(pos * BLOCK, BLOCK), BLOCK)
        zx_ref[BLOCK:, :] = -w_ref[at, :]
        top_ref[...] = l_ref[:, at]

    @pl.when(jnp.logical_not(own))
    def _():
        top_ref[...] = jnp.zeros_like(top_ref)


def factor(pos, cols_top, rhs_top, block):
    return pl.pallas_call(
        factor_kernel,
        out_shape=(f32(PIVOTS, PIVOTS), f32(PIVOTS, BLOCK), f32(BLOCK, PIVOTS), f32(2 * BLOCK, PIVOTS)),
        in_specs=[SMEM, VMEM, VMEM, VMEM],
        out_specs=(VMEM,) * 4,
        scratch_shapes=[pltpu.VMEM((PIVOTS, PIVOTS), jnp.float32)] * 2
        + [pltpu.VMEM((PIVOTS, PIVOTS), jnp.bfloat16)] * 2
        + [pltpu.VMEM((BLOCK, BLOCK), jnp.bfloat16)] * 2
        + [pltpu.VMEM((80, BLOCK), jnp.float32)],
        compiler_params=pltpu.CompilerParams(vmem_limit_bytes=48 << 20),
        cost_estimate=pl.CostEstimate(flops=40 * 10**9, bytes_accessed=16 << 20, transcendentals=0),
        name="factor",
    )(pos, cols_top, rhs_top, block)


CHIPS = SIDE * SIDE
FIRST = PIVOTS // (2 * BLOCK)
HALF = (CHIPS - FIRST) * BLOCK
WIDE = 512


def gather_half(pos, bundles, held):
    for e in range(SIDE):
        for d in range(SIDE):
            chip = place(pos, 0, e, d) // 2
            held[:, pl.ds(pl.multiple_of(chip * BLOCK, BLOCK), BLOCK)] = bundles[e][d]


HALF_SCRATCH = [pltpu.VMEM((PIVOTS, CHIPS * BLOCK), jnp.float32)]


def lanes(s, core):
    return pl.ds(pl.multiple_of(2 * BLOCK * s + BLOCK * core, BLOCK), BLOCK)


def ancestor_kernel(pos_ref, own_ref, par_ref, *refs):
    bundles, (mine_ref, other_ref, packed, total, held, more) = refs[:4], refs[4:]
    pos = pos_ref[0]
    core = pos % 2
    copies = []
    for s in range(CHIPS - FIRST):
        for side, ref in enumerate((own_ref, par_ref)):
            to = packed.at[BLOCK * side : BLOCK * (side + 1), BLOCK * s : BLOCK * (s + 1)]
            copies.append(pltpu.make_async_copy(ref.at[:, lanes(s, core)], to, more.at[2 * s + side]))
            copies[-1].start()
    gather_half(pos, bundles, held)
    for copy in copies:
        copy.wait()
    total[...] = jnp.zeros_like(total)

    def chunk(n, _):
        at = pl.ds(pl.multiple_of(n * WIDE, WIDE), WIDE)
        there = pl.ds(pl.multiple_of(FIRST * BLOCK + n * WIDE, WIDE), WIDE)
        total[...] = total[...] + mm(split(packed[:, at]), split(held[:, there]), 1, 1)
        return 0

    lax.fori_loop(0, HALF // WIDE, chunk, 0)
    mine_ref[...] = total[:BLOCK, :]
    other_ref[...] = total[BLOCK:, :]


def ancestor(pos, own, par, bundles):
    return pl.pallas_call(
        ancestor_kernel,
        out_shape=(f32(BLOCK, PIVOTS),) * 2,
        in_specs=[SMEM] + [ANY] * 2 + [VMEM] * 4,
        out_specs=(VMEM, VMEM),
        scratch_shapes=[pltpu.VMEM((2 * BLOCK, HALF), jnp.float32), pltpu.VMEM((2 * BLOCK, PIVOTS), jnp.float32)]
        + HALF_SCRATCH
        + [pltpu.SemaphoreType.DMA((2 * (CHIPS - FIRST),))],
        compiler_params=pltpu.CompilerParams(vmem_limit_bytes=32 << 20),
        cost_estimate=pl.CostEstimate(flops=3 * 10**9, bytes_accessed=12 << 20, transcendentals=0),
        name="ancestor",
    )(pos, own, par, *bundles)


def pivot_kernel(weight_ref, y1_ref, mine_ref, other_ref, w_ref, field_ref, terms_ref):
    inv = split(w_ref[...])
    inner = y1_ref[...] - mm(split(mine_ref[...] + other_ref[...]), inv, 1, 1)
    field = mm(split(inner), inv)
    field_ref[...] = field
    half = BLOCK // 2
    terms_ref[...] = weight_ref[0] * jnp.sum(field[:half] * field[half:], axis=0, keepdims=True)


def pivot(weight, y1, mine, other, w):
    return pl.pallas_call(
        pivot_kernel,
        out_shape=(f32(BLOCK, PIVOTS), f32(1, PIVOTS)),
        in_specs=[SMEM, VMEM, VMEM, VMEM, VMEM],
        out_specs=(VMEM, VMEM),
        compiler_params=pltpu.CompilerParams(vmem_limit_bytes=32 << 20),
        cost_estimate=pl.CostEstimate(flops=2 * 10**9, bytes_accessed=6 << 20, transcendentals=0),
        name="pivot",
    )(weight, y1, mine, other, w)


def update_kernel(pos_ref, first_ref, own_ref, par_ref, *refs):
    bundles, (mine_ref, other_ref, held, sems) = refs[:4], refs[4:]
    pos = pos_ref[0]
    low = first_ref[0]
    per = WIDE // BLOCK
    zx = split(jnp.concatenate([own_ref[...], par_ref[...]], 0))

    def each(act):
        for e in range(SIDE):
            for d in range(SIDE):
                slot = place(pos, 0, e, d) // 2 - low

                @pl.when((slot >= 0) & (slot < per))
                def _():
                    to = held.at[:, pl.ds(pl.multiple_of(slot * BLOCK, BLOCK), BLOCK)]
                    act(pltpu.make_async_copy(bundles[e].at[d], to, sems.at[e * SIDE + d]))

    each(lambda copy: copy.start())
    each(lambda copy: copy.wait())

    def chunk(n, _):
        at = pl.ds(pl.multiple_of(n * 256, 256), 256)
        out = mm(zx, split(held[:, at]))
        mine_ref[:, at] = out[: 2 * BLOCK]
        other_ref[:, at] = out[2 * BLOCK :]
        return 0

    lax.fori_loop(0, WIDE // 256, chunk, 0)


def update(pos, part, own, par, bundles):
    first = jnp.full((1,), FIRST + part * (WIDE // BLOCK), jnp.int32)
    return pl.pallas_call(
        update_kernel,
        out_shape=(f32(2 * BLOCK, WIDE),) * 2,
        in_specs=[SMEM, SMEM, VMEM, VMEM] + [ANY] * 4,
        out_specs=(VMEM, VMEM),
        scratch_shapes=[pltpu.VMEM((PIVOTS, WIDE), jnp.float32), pltpu.SemaphoreType.DMA((CHIPS,))],
        compiler_params=pltpu.CompilerParams(vmem_limit_bytes=20 << 20),
        cost_estimate=pl.CostEstimate(flops=2 * 10**9, bytes_accessed=5 << 20, transcendentals=0),
        name="update",
    )(pos, first, own, par, *bundles)


PARTS = HALF // WIDE


def finish_kernel(pos_ref, old_ref, *refs):
    updates, out_ref = refs[:-1], refs[-1]
    pos = pos_ref[0]
    for side in range(2):
        for part in range(PARTS):
            for t in range(WIDE // BLOCK):
                at = lanes(part * (WIDE // BLOCK) + t, (pos + side) % 2)
                out = updates[side * PARTS + part][:BLOCK, BLOCK * t : BLOCK * (t + 1)]
                out_ref[:, at] = old_ref[:, at] - out


def front_kernel(pos_ref, top_ref, old_ref, *refs):
    updates, out_ref = refs[:-1], refs[-1]
    pos = pos_ref[0]
    out_ref[:PIVOTS, :] = top_ref[...]
    own = pos < PIVOTS // BLOCK
    for side in range(2):
        core = (pos + side) % 2
        for part in range(PARTS):
            for t in range(WIDE // BLOCK):
                s = part * (WIDE // BLOCK) + t
                out = updates[side * PARTS + part][BLOCK:, BLOCK * t : BLOCK * (t + 1)]
                old = jnp.where(own, 0.0, old_ref[lanes(s, core), :])
                down = pl.ds(pl.multiple_of(PIVOTS + 2 * BLOCK * s + BLOCK * core, BLOCK), BLOCK)
                out_ref[down, :] = old - out.T


def finish(pos, rhs, updates):
    return pl.pallas_call(
        finish_kernel,
        out_shape=f32(BLOCK, REST),
        in_specs=[SMEM] + [VMEM] * (1 + len(updates)),
        out_specs=VMEM,
        compiler_params=pltpu.CompilerParams(vmem_limit_bytes=16 << 20),
        cost_estimate=pl.CostEstimate(flops=10**8, bytes_accessed=6 << 20, transcendentals=0),
        name="finish",
    )(pos, rhs, *updates)


def front(pos, top, rest, updates):
    return pl.pallas_call(
        front_kernel,
        out_shape=f32(ORDER, BLOCK),
        in_specs=[SMEM] + [VMEM] * (2 + len(updates)),
        out_specs=VMEM,
        compiler_params=pltpu.CompilerParams(vmem_limit_bytes=16 << 20),
        cost_estimate=pl.CostEstimate(flops=10**8, bytes_accessed=7 << 20, transcendentals=0),
        name="front",
    )(pos, top, rest, *updates)


PAIRS = ((1, 0, 3, 2), (3, 2, 1, 0))


def x_pairs(step):
    return [(i, i // 8 * 8 + PAIRS[step][i // 2 % SIDE] * 2 + i % 2) for i in range(32)]


def y_pairs(step):
    return [(i, PAIRS[step][i // 8] * 8 + i % 8) for i in range(32)]


def damp_pairs(step):
    return list(enumerate(PAIRS[step]))


tie = lax.optimization_barrier


def in_hbm(v):
    return pltpu.with_memory_space_constraint(v, pltpu.HBM)


def right_sides(src_index, src_amp, rec_index, resid, first, count):
    ids = jnp.arange(first, first + count, dtype=jnp.int32)
    forward = jnp.where(src_index[:, None] == ids[None, :], src_amp[:, None], 0.0)
    table = (rec_index[:, None] == ids[None, :]).astype(jnp.float32)
    adjoint = lax.dot_general(resid, table, (((0,), (0,)), ((), ())), precision=lax.Precision.HIGHEST)
    return jnp.concatenate([forward, adjoint], 0)


def per_device(
    base_front,
    child_blocks,
    child_map,
    src_index,
    src_amp,
    rec_index,
    rec_resid,
    ancestor_field,
    damp_weight,
):
    position = lax.axis_index("front")
    pos = position.reshape(1).astype(jnp.int32)
    base = base_front[0]
    maps = child_map[0]
    bundles = spread(pack(jnp.swapaxes(child_blocks[0], 1, 2)))
    base_t = base[:PIVOTS].T
    base_rows = 0.0
    for r in range(4):
        base_rows = base_rows + send(base_t[32 * r : 32 * r + 32], [(j, 4 * j + r) for j in range(8)])
    above = jnp.swapaxes(ancestor_field[0], 1, 2).reshape(BLOCK, REST)
    above_par = send(above, PARTNER)
    sides = (src_index, src_amp, rec_index, rec_resid[0])
    rhs_top = right_sides(*sides, 0, PIVOTS)
    rhs_rest = right_sides(*sides, PIVOTS, REST)
    base_top, base_rest = base[:PIVOTS], base[PIVOTS:]
    bundles, base_rows, above_par, rhs_top, rhs_rest = tie((bundles, base_rows, above_par, rhs_top, rhs_rest))
    cols_top, picks = assemble_tops(pos, maps, base_top, bundles)
    top_bundle = jnp.stack(ring(cols_top, 0))
    rows = pivot_rows(maps, base_rows, picks)
    rows, picks = tie((rows, picks))
    row_bundle = jnp.stack(ring(rows, 0))
    cols_rest = assemble_rest(maps, base_rest, picks)
    row_bundle, cols_rest, top_bundle = tie((row_bundle, cols_rest, top_bundle))
    row_own = ring(row_bundle, 1)
    row_own, top_bundle = tie((row_own, top_bundle))
    row_bundles = row_own + [send(b, PARTNER) for b in row_own]
    halves = ring(top_bundle, 1)
    w, top, y1, zx = factor(pos, cols_top, rhs_top, collect(pos, row_bundles))
    halves, w, zx = tie((halves, w, zx))
    zx_par = send(zx, PARTNER)
    mine, other = ancestor(pos, in_hbm(above), in_hbm(above_par), halves)
    field, terms = pivot(damp_weight, y1, mine, send(other, PARTNER), w)
    v = terms.reshape(8, BLOCK)
    v = v + send(v, PARTNER)
    mine, other = [], []

    def window(v, pairs, part):
        nonlocal zx
        v, zx = tie((v, zx))
        come = send(v, pairs)
        own, par = update(pos, part, zx, zx_par, halves)
        come, own, par = tie((come, own, par))
        mine.append(own)
        other.append(send(par, PARTNER))
        return v + come

    v = window(v, x_pairs(0), 0)
    v = window(v, x_pairs(1), 1)
    v = window(v, y_pairs(0), 2)
    v = v + send(v, y_pairs(1))
    updates = mine + other
    v, updates = tie((v, updates))
    come = lax.ppermute(v, "damp", damp_pairs(0))
    up = finish(pos, rhs_rest, updates)
    come, up = tie((come, up))
    v = v + come
    v, updates = tie((v, updates))
    come = lax.ppermute(v, "damp", damp_pairs(1))
    factored = front(pos, top, cols_rest, updates)
    summed = v + come
    gradient = lax.dynamic_slice_in_dim(summed.reshape(PIVOTS), position * 32, 32, 0)
    upward = jnp.swapaxes(up.reshape(2, BLOCK // 2, REST), 1, 2)
    pivot_field = jnp.swapaxes(field.reshape(2, BLOCK // 2, PIVOTS), 1, 2)
    return (factored[None], upward[None], pivot_field[None], gradient)


def solution(mesh):
    return jax.shard_map(
        per_device,
        mesh=mesh,
        in_specs=(
            P("damp", None, "front"),
            P("damp", None, None, "front"),
            P("damp", None, None),
            P("front"),
            P("front"),
            P(),
            P("damp", None, "front"),
            P("damp", None, None, "front"),
            P("damp"),
        ),
        out_specs=(
            P("damp", None, "front"),
            P("damp", None, None, "front"),
            P("damp", None, None, "front"),
            P("front"),
        ),
        check_vma=False,
    )
```
